512 devices in a mesh: section: 16 (over z_lo, y), seq: 32 (over z_hi, x, core).
Axes of the slice: x: 4, y: 8, z: 8 (z_hi: 4, z_lo: 2; z = z_hi * 2 + z_lo), core: 2. Of those that a mesh axis runs over, the one named last changes fastest.
Arguments:
- query_heads: bfloat16 [16, 4096, 4096], P('section', 'seq'), may hold values from -24 to 24
- key_heads: bfloat16 [16, 4096, 512], P('section', 'seq'), may hold values from -6 to 6
- value_heads: bfloat16 [16, 4096, 512], P('section', 'seq'), may hold values from -6 to 6
- section_cotangent: bfloat16 [16, 4096, 4096], P('section', 'seq'), may hold values from -6 to 6
- block_mask: int32 [32, 7], P('seq'), may hold values 0 or 1
Outputs:
- query_grad: bfloat16 [16, 4096, 4096], P('section', 'seq')
- key_grad: bfloat16 [16, 4096, 512], P('section', 'seq')
- value_grad: bfloat16 [16, 4096, 512], P('section', 'seq')
The draws below stay inside these ranges and needn't reach their ends.
All inputs are finite; a program needn't handle non-finite values. No bound on the sum of `block_mask` on one device may be relied on, other than what follows from the above.
Results may differ from the reference program's by a relative error of at most 0.0058.
Values may be sent and summed in bfloat16 or wider, within the bound.
No kernel may reach another device: no remote copies, remote signals or barrier semaphores. Data moves between devices by JAX's collectives and lax.ppermute only.
A program may use at most 128 MiB of HBM per device.

```python
import math
import jax
import jax.numpy as jnp
from jax import lax

HQ = 32
HK = 4
HD = 128
BLOCK = 128
W = 3
SECTIONS = 16
NBLK = 32
TOKENS = 4096


def draw_key_heads(key, part):
    normal_part = jnp.clip(jax.random.normal(jax.random.fold_in(key, 11), (SECTIONS, TOKENS, HK * HD), jnp.float32), -6.0, 6.0)
    return normal_part.astype(jnp.bfloat16)


def draw_query_heads(key, part):
    normal_part = jnp.clip(jax.random.normal(jax.random.fold_in(key, 13), (SECTIONS, TOKENS, HQ * HD), jnp.float32), -6.0, 6.0)
    return normal_part.astype(jnp.bfloat16)


def set_ends(values, own_key, least, largest):
    longest = values.shape.index(max(values.shape))
    spots = []
    for shift in (0, 1):
        where = [jax.random.randint(jax.random.fold_in(own_key, axis), (), 0, length) for axis, length in enumerate(values.shape)]
        where[longest] = (where[longest] + shift) % values.shape[longest]
        spots.append(tuple(where))
    return values.at[spots[0]].set(least).at[spots[1]].set(largest)


def shard_levels(rng, extent, pieces, low, top_value):
    gain, own = 1.0, jax.random.fold_in(rng, 6)
    for position, shards_of in pieces:
        steps = jnp.exp(jax.random.uniform(jax.random.fold_in(own, position), (shards_of,), jnp.float32, low / len(pieces), top_value / len(pieces)))
        gain = gain * jnp.repeat(steps, extent[position] // shards_of).reshape([-1 if axis == position else 1 for axis in range(len(extent))])
    return gain


def bell_draw(key, dims, deviation, reach, split=(), kind=jnp.bfloat16):
    entries = jax.random.normal(key, dims, jnp.float32) * deviation
    if len(split) > 0:
        entries = shard_levels(key, dims, split, -0.22, 0.18) * entries
    return jnp.clip(entries, min=-reach, max=reach).astype(kind)


def setup_inputs(seed: int = 0) -> dict:
    arg_keys = jax.random.split(jax.random.key(seed), 6)
    query_heads = draw_query_heads(jax.random.fold_in(arg_keys[5], 71), 0)
    key_heads = draw_key_heads(jax.random.fold_in(arg_keys[5], 71), 0)
    value_heads = bell_draw(arg_keys[2], (SECTIONS, TOKENS, HK * HD), 1.0, 6.0, ((0, 16), (1, 32)))
    section_cotangent = bell_draw(arg_keys[3], (SECTIONS, TOKENS, HQ * HD), 1.0, 6.0, ((0, 16), (1, 32)))
    block_mask = set_ends((jax.random.randint(arg_keys[4], (NBLK, 2 * W + 1), 0, 2) < 1).astype(jnp.int32), jax.random.fold_in(arg_keys[4], 1), 0, 1)
    return {"query_heads": query_heads, "key_heads": key_heads, "value_heads": value_heads, "section_cotangent": section_cotangent, "block_mask": block_mask}


def block_grads(query_block, near_keys, near_values, grad_block, flag_row):
    groups = HQ // HK
    window_len = 2 * W + 1
    score_scale = 1.0 / math.sqrt(HD)
    scores = jnp.einsum('qhgd,jkhd->hgqjk', query_block, near_keys) * score_scale
    scores = jnp.where(flag_row[:, None], scores, -jnp.inf)
    flat = scores.reshape(HK, groups, BLOCK, window_len * BLOCK)
    row_peak = lax.optimization_barrier(jnp.max(flat, axis=-1, keepdims=True))
    weights = jnp.exp(flat - row_peak)
    probs = (weights / lax.optimization_barrier(jnp.sum(weights, axis=-1, keepdims=True))).reshape(scores.shape)
    grad_probs = jnp.einsum('qhgd,jkhd->hgqjk', grad_block, near_values)
    row_delta = lax.optimization_barrier(jnp.sum(probs * grad_probs, axis=(3, 4), keepdims=True))
    dscore = (probs * (grad_probs - row_delta)).astype(jnp.bfloat16)
    probs_b = probs.astype(jnp.bfloat16)
    dscore, probs_b = lax.optimization_barrier((dscore, probs_b))
    dscore_wide = dscore.astype(jnp.float32)
    probs_wide = probs_b.astype(jnp.float32)
    query_part = (jnp.einsum('hgqjk,jkhd->qhgd', dscore_wide, near_keys) * score_scale).astype(jnp.bfloat16)
    key_part = (jnp.einsum('hgqjk,qhgd->jkhd', dscore_wide, query_block) * score_scale).astype(jnp.bfloat16)
    value_part = jnp.einsum('hgqjk,qhgd->jkhd', probs_wide, grad_block).astype(jnp.bfloat16)
    key_part, value_part = lax.optimization_barrier((key_part, value_part))
    return (query_part.reshape(BLOCK, HQ * HD), key_part, value_part)

def reference(query_heads, key_heads, value_heads, section_cotangent, block_mask):
    groups = HQ // HK
    window_len = 2 * W + 1
    offsets = jnp.arange(window_len, dtype=jnp.int32) - W
    block_ids = jnp.arange(NBLK, dtype=jnp.int32)
    targets = block_ids[:, None] + offsets[None, :]
    inside = (targets >= 0) & (targets < NBLK)
    active = inside & ((offsets[None, :] == 0) | (block_mask == 1))
    clipped = jnp.clip(targets, 0, NBLK - 1).astype(jnp.int32)
    keep_mask = inside.astype(jnp.float32)[:, :, None, None, None]
    grad_out = jnp.roll(section_cotangent, -1, axis=0)

    def one_section(section_items):
        queries, key_rows, value_rows, grad_rows = section_items
        q_four = queries.astype(jnp.float32).reshape(NBLK, BLOCK, HK, groups, HD)
        g_four = grad_rows.astype(jnp.float32).reshape(NBLK, BLOCK, HK, groups, HD)
        k_four = key_rows.astype(jnp.float32).reshape(NBLK, BLOCK, HK, HD)
        v_four = value_rows.astype(jnp.float32).reshape(NBLK, BLOCK, HK, HD)

        def one_block(block_items):
            query_block, grad_block, index_row, flag_row = block_items
            return block_grads(query_block, k_four[index_row], v_four[index_row], grad_block, flag_row)
        query_grad, key_parts, value_parts = lax.map(one_block, (q_four, g_four, clipped, active))
        key_total = jnp.zeros((NBLK, BLOCK, HK, HD), jnp.float32).at[clipped].add(key_parts.astype(jnp.float32) * keep_mask)
        value_total = jnp.zeros((NBLK, BLOCK, HK, HD), jnp.float32).at[clipped].add(value_parts.astype(jnp.float32) * keep_mask)
        return (query_grad.reshape(TOKENS, HQ * HD), key_total.astype(jnp.bfloat16).reshape(TOKENS, HK * HD), value_total.astype(jnp.bfloat16).reshape(TOKENS, HK * HD))
    query_grad, key_grad, value_grad = lax.map(one_section, (query_heads, key_heads, value_heads, grad_out))
    return (query_grad, key_grad, value_grad)
```

```python
import functools
import math

import jax
import jax.numpy as jnp
from jax import lax
from jax.experimental import pallas as pl
from jax.experimental.pallas import tpu as pltpu
from jax.sharding import PartitionSpec as P

HQ, HK, HD, W = 32, 4, 128, 3
BL = 128
G = HQ // HK
NS = 7
SCALE = 1.0 / math.sqrt(HD)
LOG2E = 1.4426950408889634

NT = (((1,), (1,)), ((), ()))
NN = (((1,), (0,)), ((), ()))


def body(flags, q, g, own_k, own_v, left, right, far, mate, dq, parts, to_mate, to_far, kc, vc, kt, pairs=4):
    lw = G * BL // pairs
    kc[0:128] = own_k[...]
    vc[0:128] = own_v[...]
    for s, ref in ((1, left), (2, right), (3, far)):
        kc[s * BL:(s + 1) * BL] = ref[0]
        vc[s * BL:(s + 1) * BL] = ref[1]
    kc[4 * BL:] = mate[0]
    vc[4 * BL:] = mate[1]
    for s in range(NS):
        kt[:, s * BL:(s + 1) * BL] = kc[s * BL:(s + 1) * BL, :].T
    dk = dv = None
    for t in range(pairs):
        n = lw // HD
        cols = [slice((t * n + i) * HD, (t * n + i + 1) * HD) for i in range(n)]
        qp = jnp.concatenate([q[:, c] for c in cols], axis=0)
        gp = jnp.concatenate([g[:, c] for c in cols], axis=0)
        s = lax.dot_general(kc[...], qp, NT, preferred_element_type=jnp.float32)
        s = jnp.concatenate([jnp.where(flags[i] != 0, s[i * BL:(i + 1) * BL], -jnp.inf) for i in range(NS)], axis=0)
        m = jnp.max(s, axis=0, keepdims=True)
        e = jnp.exp2((s - m) * (SCALE * LOG2E))
        inv = 1.0 / jnp.sum(e, axis=0, keepdims=True)
        p = e * inv
        dp = lax.dot_general(vc[...], gp, NT, preferred_element_type=jnp.float32)
        delta = jnp.sum(p * dp, axis=0, keepdims=True)
        ds = (p * (dp - delta)).astype(jnp.bfloat16)
        pb = p.astype(jnp.bfloat16)
        a = lax.dot_general(pb, gp, NN, preferred_element_type=jnp.float32)
        b = lax.dot_general(ds, qp, NN, preferred_element_type=jnp.float32)
        dv = a if dv is None else dv + a
        dk = b if dk is None else dk + b
        dqt = lax.dot_general(kt[...], ds, NN, preferred_element_type=jnp.float32)
        for i, c in enumerate(cols):
            dq[:, c] = (dqt[:, i * BL:(i + 1) * BL].T * SCALE).astype(jnp.bfloat16)
    dk = dk * SCALE
    parts[0] = dk[:3 * BL]
    parts[1] = dv[:3 * BL]
    to_far[0] = dk[3 * BL:4 * BL].astype(jnp.bfloat16)
    to_far[1] = dv[3 * BL:4 * BL].astype(jnp.bfloat16)
    to_mate[0] = dk[4 * BL:].astype(jnp.bfloat16)
    to_mate[1] = dv[4 * BL:].astype(jnp.bfloat16)


def attn(flags, q, g, k, v, left, right, far, mate, pairs=4):
    b16 = jnp.bfloat16
    col = lambda h: (0, h)
    col3 = lambda h: (0, 0, h)
    return pl.pallas_call(
        functools.partial(body, pairs=pairs),
        grid=(HK,),
        in_specs=[
            pl.BlockSpec(memory_space=pltpu.SMEM),
            pl.BlockSpec((BL, G * HD), col),
            pl.BlockSpec((BL, G * HD), col),
            pl.BlockSpec((BL, HD), col),
            pl.BlockSpec((BL, HD), col),
            pl.BlockSpec((2, BL, HD), col3),
            pl.BlockSpec((2, BL, HD), col3),
            pl.BlockSpec((2, BL, HD), col3),
            pl.BlockSpec((2, 3 * BL, HD), col3),
        ],
        out_specs=[
            pl.BlockSpec((BL, G * HD), col),
            pl.BlockSpec((2, 3 * BL, HD), col3),
            pl.BlockSpec((2, 3 * BL, HD), col3),
            pl.BlockSpec((2, BL, HD), col3),
        ],
        out_shape=[
            jax.ShapeDtypeStruct((BL, HQ * HD), b16),
            jax.ShapeDtypeStruct((2, 3 * BL, HK * HD), jnp.float32),
            jax.ShapeDtypeStruct((2, 3 * BL, HK * HD), b16),
            jax.ShapeDtypeStruct((2, BL, HK * HD), b16),
        ],
        scratch_shapes=[
            pltpu.VMEM((NS * BL, HD), b16),
            pltpu.VMEM((NS * BL, HD), b16),
            pltpu.VMEM((HD, NS * BL), b16),
        ],
        compiler_params=pltpu.CompilerParams(vmem_limit_bytes=40 << 20),
        name="attention_backward",
    )(flags, q, g, k, v, left, right, far, mate)


def shift_pairs(count, by):
    return [(i, i + by) for i in range(count) if 0 <= i + by < count]


def mate_pairs(count):
    return [(i, i ^ 1) for i in range(count)]


def far_pairs(count):
    return [(i, i + (3 if i % 2 else -3)) for i in range(count) if 0 <= i + (3 if i % 2 else -3) < count]


def slot_flags(mask_row, index, count):
    odd = index % 2
    sign = 1 - 2 * odd
    offsets = [0, -2, 2, -3 * sign, sign, sign - 2, sign + 2]
    flags = [jnp.int32(1)]
    for offset in offsets[1:]:
        inside = (index + offset >= 0) & (index + offset < count)
        on = jnp.sum(jnp.where(jnp.arange(2 * W + 1) == offset + W, mask_row, 0)) == 1
        flags.append((inside & on).astype(jnp.int32))
    return jnp.stack(flags)


def shards(query_heads, key_heads, value_heads, section_cotangent, block_mask):
    sections = lax.axis_size("section")
    count = lax.axis_size("seq")
    index = lax.axis_index("seq")
    grad_out = lax.ppermute(
        section_cotangent, "section", [(i, (i - 1) % sections) for i in range(sections)]
    )
    own = jnp.stack([key_heads[0], value_heads[0]])
    left = lax.ppermute(own, "seq", shift_pairs(count, 2))
    right = lax.ppermute(own, "seq", shift_pairs(count, -2))
    far = lax.ppermute(own, "seq", far_pairs(count))
    mate = lax.ppermute(jnp.concatenate([own, left, right], axis=1), "seq", mate_pairs(count))
    flags = slot_flags(block_mask[0], index, count)
    query_grad, parts, to_mate, to_far = attn(
        flags, query_heads[0], grad_out[0], key_heads[0], value_heads[0], left, right, far, mate, pairs=1
    )
    from_mate = lax.ppermute(to_mate, "seq", mate_pairs(count))
    sums = parts + from_mate.astype(jnp.float32)
    back_left = lax.ppermute(sums[:, BL : 2 * BL].astype(jnp.bfloat16), "seq", shift_pairs(count, -2))
    back_right = lax.ppermute(sums[:, 2 * BL :].astype(jnp.bfloat16), "seq", shift_pairs(count, 2))
    back_far = lax.ppermute(to_far, "seq", far_pairs(count))
    total = sums[:, :BL]
    for arrived in (back_left, back_right, back_far):
        total = total + arrived.astype(jnp.float32)
    total = total.astype(jnp.bfloat16)
    return query_grad[None], total[0][None], total[1][None]


def solution(mesh):
    in_specs = (
        P("section", "seq", None),
        P("section", "seq", None),
        P("section", "seq", None),
        P("section", "seq", None),
        P("seq", None),
    )
    out_specs = (P("section", "seq", None), P("section", "seq", None), P("section", "seq", None))
    return jax.shard_map(shards, mesh=mesh, in_specs=in_specs, out_specs=out_specs, check_vma=False)
```

```python
import functools
import math

import jax
import jax.numpy as jnp
from jax import lax
from jax.experimental import pallas as pl
from jax.experimental.pallas import tpu as pltpu
from jax.sharding import PartitionSpec as P

HQ, HK, HD, W = 32, 4, 128, 3
BL = 128
G = HQ // HK
NS = 2 * W + 1
SCALE = 1.0 / math.sqrt(HD)
LOG2E = math.log2(math.e)
NT = (((1,), (1,)), ((), ()))
NN = (((1,), (0,)), ((), ()))
F32, B16 = jnp.float32, jnp.bfloat16


def slot_offsets(odd):
    sign = 1 - 2 * odd
    return [0, -2, 2, -3 * sign, sign, sign - 2, sign + 2]


def backward_body(n_grads, n_kept, *refs):
    mask, q = refs[:2]
    grads = refs[2 : 2 + n_grads]
    own, left, right, far, mate = refs[2 + n_grads : 7 + n_grads]
    dq, parts, to_mate, to_far, kc, vc, kt = refs[7 + n_grads + n_kept :]
    index = lax.axis_index("seq")
    count = lax.axis_size("seq")
    on = [None]
    for offset in slot_offsets(index % 2)[1:]:
        inside = (index + offset >= 0) & (index + offset < count)
        on.append(inside & (mask[0, offset + W] == 1))
    row = 0
    for ref in (own, left, right, far, mate):
        n = ref.shape[1]
        kc[row : row + n] = ref[0]
        vc[row : row + n] = ref[1]
        row += n
    for s in range(NS):
        kt[:, s * BL : (s + 1) * BL] = kc[s * BL : (s + 1) * BL, :].T
    cols = [slice(i * HD, (i + 1) * HD) for i in range(G)]
    qp = jnp.concatenate([q[:, c] for c in cols], axis=0)
    gp = jnp.concatenate([grads[0][:, c] for c in cols], axis=0)
    for more in grads[1:]:
        gp = gp + jnp.concatenate([more[:, c] for c in cols], axis=0)
    s = lax.dot_general(kc[...], qp, NT, preferred_element_type=F32)
    pieces = [s[i * BL : (i + 1) * BL] for i in range(NS)]
    pieces = [p if f is None else jnp.where(f, p, -jnp.inf) for p, f in zip(pieces, on)]
    s = jnp.concatenate(pieces, axis=0)
    m = jnp.max(s, axis=0, keepdims=True)
    e = jnp.exp2((s - m) * (SCALE * LOG2E))
    p = e * (1.0 / jnp.sum(e, axis=0, keepdims=True))
    dp = lax.dot_general(vc[...], gp, NT, preferred_element_type=F32)
    delta = jnp.sum(p * dp, axis=0, keepdims=True)
    ds = (p * (dp - delta)).astype(B16)
    dv = lax.dot_general(p.astype(B16), gp, NN, preferred_element_type=F32)
    dk = lax.dot_general(ds, qp, NN, preferred_element_type=F32) * SCALE
    dqt = lax.dot_general(kt[...], ds, NN, preferred_element_type=F32)
    for i, c in enumerate(cols):
        dq[:, c] = (dqt[:, c].T * SCALE).astype(B16)
    for i, d in enumerate((dk, dv)):
        parts[i] = d[: 3 * BL]
        to_far[i] = d[3 * BL : 4 * BL].astype(B16)
        to_mate[i] = d[4 * BL :].astype(B16)


def attention_backward(mask, q, grads, slots, first, heads, kept):
    at = lambda h: (0, h + first)
    at3 = lambda h: (0, 0, h + first)
    here = lambda h: (0, h)
    width = HK * HD
    shapes = [((BL, HQ * HD), B16), ((2, 3 * BL, width), F32), ((2, 3 * BL, width), B16), ((2, BL, width), B16)]
    n_in = 2 + len(grads) + len(slots)
    return pl.pallas_call(
        functools.partial(backward_body, len(grads), len(kept)),
        grid=(heads,),
        in_specs=[pl.BlockSpec(memory_space=pltpu.SMEM), pl.BlockSpec((BL, G * HD), at)]
        + [pl.BlockSpec((BL, G * HD), here) for _ in grads]
        + [pl.BlockSpec((2, x.shape[1], HD), at3) for x in slots]
        + [pl.BlockSpec(memory_space=pl.ANY) for _ in kept],
        out_specs=[pl.BlockSpec((BL, G * HD), at)] + [pl.BlockSpec((2, s[1], HD), at3) for s, _ in shapes[1:]],
        out_shape=[jax.ShapeDtypeStruct(s, d) for s, d in shapes],
        scratch_shapes=[pltpu.VMEM((NS * BL, HD), B16), pltpu.VMEM((NS * BL, HD), B16), pltpu.VMEM((HD, NS * BL), B16)],
        input_output_aliases={n_in + i: i for i in range(len(kept))},
        compiler_params=pltpu.CompilerParams(vmem_limit_bytes=32 << 20),
        cost_estimate=pl.CostEstimate(flops=heads << 30, bytes_accessed=heads << 20, transcendentals=heads << 20),
        name="attention_backward",
    )(mask, q, *grads, *slots, *kept)


def join_body(k, v, out):
    out[0] = k[...]
    out[1] = v[...]


def join(k, v):
    return pl.pallas_call(
        join_body,
        out_shape=jax.ShapeDtypeStruct((2, *k.shape), k.dtype),
        compiler_params=pltpu.CompilerParams(vmem_limit_bytes=4 << 20),
        name="join",
    )(k, v)


def relay_body(own, left, right, bundle, onward):
    odd = lax.axis_index("seq") % 2 == 1
    for i, ref in enumerate((own, left, right)):
        bundle[:, i * BL : (i + 1) * BL] = ref[...]

    @pl.when(odd)
    def _():
        onward[...] = left[...]

    @pl.when(jnp.logical_not(odd))
    def _():
        onward[...] = right[...]


def relay(own, left, right):
    n, rows, cols = left.shape
    return pl.pallas_call(
        relay_body,
        out_shape=[
            jax.ShapeDtypeStruct((n, 3 * rows, cols), left.dtype),
            jax.ShapeDtypeStruct(left.shape, left.dtype),
        ],
        compiler_params=pltpu.CompilerParams(vmem_limit_bytes=8 << 20),
        name="relay",
    )(own, left, right)


def hold_body(x, out):
    pass


def hold(x):
    return pl.pallas_call(
        hold_body,
        in_specs=[pl.BlockSpec(memory_space=pl.ANY)],
        out_specs=pl.BlockSpec(memory_space=pl.ANY),
        out_shape=jax.ShapeDtypeStruct(x.shape, x.dtype),
        input_output_aliases={0: 0},
        compiler_params=pltpu.CompilerParams(vmem_limit_bytes=1 << 20),
        cost_estimate=pl.CostEstimate(flops=1 << 33, bytes_accessed=0, transcendentals=0),
        name="hold",
    )(x)


def shift_pairs(count, by):
    return [(i, i + by) for i in range(count) if 0 <= i + by < count]


def mate_pairs(count):
    return [(i, i ^ 1) for i in range(count)]


def edge_pairs(count):
    return [(i, j) for i in range(1, count - 1, 2) for j in (i + 1,)] + [(i + 1, i) for i in range(1, count - 1, 2)]


def shards(query_heads, key_heads, value_heads, section_cotangent, block_mask):
    sections = lax.axis_size("section")
    turn = sections // 2
    count = lax.axis_size("seq")
    odd = lax.axis_index("seq") % 2 == 1
    half = HQ * HD // 2
    cot = section_cotangent[0]
    straight = [(i, i - 1) for i in range(sections) if i % turn]
    low, high = cot[:, :half], cot[:, half:]
    grad_low = hold(lax.ppermute(low, "section", [(i, (i - 1) % sections) for i in range(sections)]))
    turned = lax.ppermute(high, "section", [(0, turn), (turn, 0)])
    own = join(key_heads[0], value_heads[0])
    left = lax.ppermute(own, "seq", shift_pairs(count, 2))
    right = lax.ppermute(own, "seq", shift_pairs(count, -2))
    grad_high = lax.ppermute(high, "section", straight)
    bundle, onward = relay(own, left, right)
    far = lax.ppermute(onward, "seq", edge_pairs(count))
    mate = lax.ppermute(bundle, "seq", mate_pairs(count))
    grad_wrap = lax.ppermute(turned, "section", [(0, turn - 1), (turn, sections - 1)])
    slots = (own, left, right, far, mate)
    kept = attention_backward(block_mask, query_heads[0], (grad_low,), slots, 0, 2, ())
    query_grad, parts, to_mate, to_far = attention_backward(
        block_mask, query_heads[0], (grad_high, grad_wrap), slots, 2, 2, kept
    )
    from_far = lax.ppermute(to_far, "seq", edge_pairs(count)).astype(F32)
    from_mate = lax.ppermute(to_mate, "seq", mate_pairs(count)).astype(F32)
    sums = parts + from_mate
    to_left = (sums[:, BL : 2 * BL] + jnp.where(odd, from_far, 0.0)).astype(B16)
    to_right = (sums[:, 2 * BL :] + jnp.where(odd, 0.0, from_far)).astype(B16)
    back_left = lax.ppermute(to_left, "seq", shift_pairs(count, -2))
    back_right = lax.ppermute(to_right, "seq", shift_pairs(count, 2))
    total = (sums[:, :BL] + back_left.astype(F32) + back_right.astype(F32)).astype(B16)
    return query_grad[None], total[0][None], total[1][None]


def solution(mesh):
    in_specs = (
        P("section", "seq", None),
        P("section", "seq", None),
        P("section", "seq", None),
        P("section", "seq", None),
        P("seq", None),
    )
    out_specs = (P("section", "seq", None), P("section", "seq", None), P("section", "seq", None))
    return jax.shard_map(shards, mesh=mesh, in_specs=in_specs, out_specs=out_specs, check_vma=False)
```

```python
import functools
import math

import jax
import jax.numpy as jnp
from jax import lax
from jax.experimental import pallas as pl
from jax.experimental.pallas import tpu as pltpu
from jax.sharding import PartitionSpec as P

HQ, HK, HD, W = 32, 4, 128, 3
BL = 128
ROW = 8
G = HQ // HK
NS = 2 * W + 1
SCALE = 1.0 / math.sqrt(HD)
LOG2E = math.log2(math.e)
NT = (((1,), (1,)), ((), ()))
NN = (((1,), (0,)), ((), ()))
F32, B16 = jnp.float32, jnp.bfloat16


def slot_offsets(odd):
    sign = 1 - 2 * odd
    return [0, -2, 2, -3 * sign, sign, sign - 2, sign + 2]


def at_corner(index):
    place = index % ROW
    return (place == 0) | (place == ROW - 1)


def backward_body(n_grads, n_kept, *refs):
    mask, q = refs[:2]
    grads = refs[2 : 2 + n_grads]
    own, left, right, far, far_row, mate = refs[2 + n_grads : 8 + n_grads]
    dq, parts, to_mate, to_far, kc, vc, kt = refs[8 + n_grads + n_kept :]
    index = lax.axis_index("seq")
    count = lax.axis_size("seq")
    on = [None]
    for offset in slot_offsets(index % 2)[1:]:
        inside = (index + offset >= 0) & (index + offset < count)
        on.append(inside & (mask[0, offset + W] == 1))
    corner = at_corner(index)

    def place(ref, row):
        kc[row : row + ref.shape[1]] = ref[0]
        vc[row : row + ref.shape[1]] = ref[1]

    for i, ref in enumerate((own, left, right)):
        place(ref, i * BL)
    pl.when(corner)(lambda: place(far_row, 3 * BL))
    pl.when(jnp.logical_not(corner))(lambda: place(far, 3 * BL))
    place(mate, 4 * BL)
    for s in range(NS):
        kt[:, s * BL : (s + 1) * BL] = kc[s * BL : (s + 1) * BL, :].T
    cols = [slice(i * HD, (i + 1) * HD) for i in range(G)]
    qp = jnp.concatenate([q[:, c] for c in cols], axis=0)
    gp = jnp.concatenate([grads[0][:, c] for c in cols], axis=0)
    for more in grads[1:]:
        gp = gp + jnp.concatenate([more[:, c] for c in cols], axis=0)
    s = lax.dot_general(kc[...], qp, NT, preferred_element_type=F32)
    pieces = [s[i * BL : (i + 1) * BL] for i in range(NS)]
    pieces = [p if f is None else jnp.where(f, p, -jnp.inf) for p, f in zip(pieces, on)]
    s = jnp.concatenate(pieces, axis=0)
    m = jnp.max(s, axis=0, keepdims=True)
    e = jnp.exp2((s - m) * (SCALE * LOG2E))
    p = e * (1.0 / jnp.sum(e, axis=0, keepdims=True))
    dp = lax.dot_general(vc[...], gp, NT, preferred_element_type=F32)
    delta = jnp.sum(p * dp, axis=0, keepdims=True)
    ds = (p * (dp - delta)).astype(B16)
    dv = lax.dot_general(p.astype(B16), gp, NN, preferred_element_type=F32)
    dk = lax.dot_general(ds, qp, NN, preferred_element_type=F32) * SCALE
    dqt = lax.dot_general(kt[...], ds, NN, preferred_element_type=F32)
    for i, c in enumerate(cols):
        dq[:, c] = (dqt[:, c].T * SCALE).astype(B16)
    for i, d in enumerate((dk, dv)):
        parts[i] = d[: 3 * BL]
        to_far[i] = d[3 * BL : 4 * BL].astype(B16)
        to_mate[i] = d[4 * BL :].astype(B16)


def attention_backward(mask, q, grads, slots, first, heads, kept):
    at = lambda h: (0, h + first)
    at3 = lambda h: (0, 0, h + first)
    here = lambda h: (0, h)
    width = HK * HD
    shapes = [((BL, HQ * HD), B16), ((2, 3 * BL, width), F32), ((2, 3 * BL, width), B16), ((2, BL, width), B16)]
    n_in = 2 + len(grads) + len(slots)
    return pl.pallas_call(
        functools.partial(backward_body, len(grads), len(kept)),
        grid=(heads,),
        in_specs=[pl.BlockSpec(memory_space=pltpu.SMEM), pl.BlockSpec((BL, G * HD), at)]
        + [pl.BlockSpec((BL, G * HD), here) for _ in grads]
        + [pl.BlockSpec((2, x.shape[1], HD), at3) for x in slots]
        + [pl.BlockSpec(memory_space=pl.ANY) for _ in kept],
        out_specs=[pl.BlockSpec((BL, G * HD), at)] + [pl.BlockSpec((2, s[1], HD), at3) for s, _ in shapes[1:]],
        out_shape=[jax.ShapeDtypeStruct(s, d) for s, d in shapes],
        scratch_shapes=[pltpu.VMEM((NS * BL, HD), B16), pltpu.VMEM((NS * BL, HD), B16), pltpu.VMEM((HD, NS * BL), B16)],
        input_output_aliases={n_in + i: i for i in range(len(kept))},
        compiler_params=pltpu.CompilerParams(vmem_limit_bytes=32 << 20),
        cost_estimate=pl.CostEstimate(flops=heads << 30, bytes_accessed=heads << 20, transcendentals=heads << 20),
        name="attention_backward",
    )(mask, q, *grads, *slots, *kept)


def join_body(k, v, out):
    out[0] = k[...]
    out[1] = v[...]


def join(k, v):
    return pl.pallas_call(
        join_body,
        out_shape=jax.ShapeDtypeStruct((2, *k.shape), k.dtype),
        compiler_params=pltpu.CompilerParams(vmem_limit_bytes=4 << 20),
        name="join",
    )(k, v)


def bundle_body(own, left, right, out):
    for i, ref in enumerate((own, left, right)):
        out[:, i * BL : (i + 1) * BL] = ref[...]


def bundle(own, left, right):
    n, rows, cols = own.shape
    return pl.pallas_call(
        bundle_body,
        out_shape=jax.ShapeDtypeStruct((n, 3 * rows, cols), own.dtype),
        compiler_params=pltpu.CompilerParams(vmem_limit_bytes=8 << 20),
        name="bundle",
    )(own, left, right)


def hold_body(*refs):
    pass


def hold(*arrays):
    anywhere = [pl.BlockSpec(memory_space=pl.ANY) for _ in arrays]
    return pl.pallas_call(
        hold_body,
        in_specs=anywhere,
        out_specs=anywhere,
        out_shape=[jax.ShapeDtypeStruct(x.shape, x.dtype) for x in arrays],
        input_output_aliases={i: i for i in range(len(arrays))},
        compiler_params=pltpu.CompilerParams(vmem_limit_bytes=1 << 20),
        cost_estimate=pl.CostEstimate(flops=1 << 34, bytes_accessed=0, transcendentals=0),
        name="hold",
    )(*arrays)


def shift_pairs(count, by):
    return [(i, i + by) for i in range(count) if 0 <= i + by < count]


def mate_pairs(count):
    return [(i, i ^ 1) for i in range(count)]


def far_hops(count):
    first, second = [], []
    for i in range(count):
        j = i + 3 if i % 2 else i - 3
        if not 0 <= j < count:
            continue
        if j // ROW != i // ROW and j % ROW in (0, ROW - 1):
            via = j // ROW * ROW + ROW - 1 - j % ROW
            first.append((i, via))
            second.append((via, j))
        else:
            first.append((i, j))
    return first, second


def shards(query_heads, key_heads, value_heads, section_cotangent, block_mask):
    sections = lax.axis_size("section")
    count = lax.axis_size("seq")
    corner = at_corner(lax.axis_index("seq"))
    half = HQ * HD // 2
    cot = section_cotangent[0]
    before = [(i, (i - 1) % sections) for i in range(sections)]
    first, second = far_hops(count)
    own = join(key_heads[0], value_heads[0])
    left = lax.ppermute(own, "seq", shift_pairs(count, 2))
    right = lax.ppermute(own, "seq", shift_pairs(count, -2))
    far = lax.ppermute(own, "seq", first)
    (grad_low,) = hold(lax.ppermute(cot[:, :half], "section", before))
    grad_high = lax.ppermute(cot[:, half:], "section", before)
    mate = lax.ppermute(bundle(own, left, right), "seq", mate_pairs(count))
    far_row = lax.ppermute(far, "seq", second)
    slots = (own, left, right, far, far_row, mate)
    kept = attention_backward(block_mask, query_heads[0], (grad_low,), slots, 0, 2, ())
    query_grad, parts, to_mate, to_far = attention_backward(
        block_mask, query_heads[0], (grad_high,), slots, 2, 2, kept
    )
    back_far = lax.ppermute(to_far, "seq", first)
    sums = parts + lax.ppermute(to_mate, "seq", mate_pairs(count)).astype(F32)
    back_left, back_right = hold(
        lax.ppermute(sums[:, BL : 2 * BL].astype(B16), "seq", shift_pairs(count, -2)),
        lax.ppermute(sums[:, 2 * BL :].astype(B16), "seq", shift_pairs(count, 2)),
    )
    back_row = lax.ppermute(back_far, "seq", second)
    total = sums[:, :BL] + back_left.astype(F32) + back_right.astype(F32)
    total = (total + jnp.where(corner, back_row, back_far).astype(F32)).astype(B16)
    return query_grad[None], total[0][None], total[1][None]


def solution(mesh):
    in_specs = (
        P("section", "seq", None),
        P("section", "seq", None),
        P("section", "seq", None),
        P("section", "seq", None),
        P("seq", None),
    )
    out_specs = (P("section", "seq", None), P("section", "seq", None), P("section", "seq", None))
    return jax.shard_map(shards, mesh=mesh, in_specs=in_specs, out_specs=out_specs, check_vma=False)
```

```python
import functools
import math

import jax
import jax.numpy as jnp
from jax import lax
from jax.experimental import pallas as pl
from jax.experimental.pallas import tpu as pltpu
from jax.sharding import PartitionSpec as P

HQ, HK, HD, W = 32, 4, 128, 3
BL = 128
G = HQ // HK
NS = 2 * W + 1
SCALE = 1.0 / math.sqrt(HD)
LOG2E = math.log2(math.e)
NT = (((1,), (1,)), ((), ()))
NN = (((1,), (0,)), ((), ()))
F32, B16 = jnp.float32, jnp.bfloat16


def slot_offsets(odd):
    sign = 1 - 2 * odd
    return [0, -2, 2, -3 * sign, sign, sign - 2, sign + 2]


def backward_body(n_grads, n_kept, *refs):
    mask, q = refs[:2]
    grads = refs[2 : 2 + n_grads]
    own, left, right, far, mate = refs[2 + n_grads : 7 + n_grads]
    dq, parts, to_mate, to_far, kc, vc, kt = refs[7 + n_grads + n_kept :]
    index = lax.axis_index("seq")
    count = lax.axis_size("seq")
    on = [None]
    for offset in slot_offsets(index % 2)[1:]:
        inside = (index + offset >= 0) & (index + offset < count)
        on.append(inside & (mask[0, offset + W] == 1))
    row = 0
    for ref in (own, left, right, far, mate):
        n = ref.shape[1]
        kc[row : row + n] = ref[0]
        vc[row : row + n] = ref[1]
        row += n
    for s in range(NS):
        kt[:, s * BL : (s + 1) * BL] = kc[s * BL : (s + 1) * BL, :].T
    cols = [slice(i * HD, (i + 1) * HD) for i in range(G)]
    qp = jnp.concatenate([q[:, c] for c in cols], axis=0)
    gp = jnp.concatenate([grads[0][:, c] for c in cols], axis=0)
    for more in grads[1:]:
        gp = gp + jnp.concatenate([more[:, c] for c in cols], axis=0)
    s = lax.dot_general(kc[...], qp, NT, preferred_element_type=F32)
    pieces = [s[i * BL : (i + 1) * BL] for i in range(NS)]
    pieces = [p if f is None else jnp.where(f, p, -jnp.inf) for p, f in zip(pieces, on)]
    s = jnp.concatenate(pieces, axis=0)
    m = jnp.max(s, axis=0, keepdims=True)
    e = jnp.exp2((s - m) * (SCALE * LOG2E))
    p = e * (1.0 / jnp.sum(e, axis=0, keepdims=True))
    dp = lax.dot_general(vc[...], gp, NT, preferred_element_type=F32)
    delta = jnp.sum(p * dp, axis=0, keepdims=True)
    ds = (p * (dp - delta)).astype(B16)
    dv = lax.dot_general(p.astype(B16), gp, NN, preferred_element_type=F32)
    dk = lax.dot_general(ds, qp, NN, preferred_element_type=F32) * SCALE
    dqt = lax.dot_general(kt[...], ds, NN, preferred_element_type=F32)
    for i, c in enumerate(cols):
        dq[:, c] = (dqt[:, c].T * SCALE).astype(B16)
    for i, d in enumerate((dk, dv)):
        parts[i] = d[: 3 * BL]
        to_far[i] = d[3 * BL : 4 * BL].astype(B16)
        to_mate[i] = d[4 * BL :].astype(B16)


def attention_backward(mask, q, grads, slots, first, heads, kept):
    at = lambda h: (0, h + first)
    at3 = lambda h: (0, 0, h + first)
    here = lambda h: (0, h)
    width = HK * HD
    shapes = [((BL, HQ * HD), B16), ((2, 3 * BL, width), F32), ((2, 3 * BL, width), B16), ((2, BL, width), B16)]
    n_in = 2 + len(grads) + len(slots)
    return pl.pallas_call(
        functools.partial(backward_body, len(grads), len(kept)),
        grid=(heads,),
        in_specs=[pl.BlockSpec(memory_space=pltpu.SMEM), pl.BlockSpec((BL, G * HD), at)]
        + [pl.BlockSpec((BL, G * HD), here) for _ in grads]
        + [pl.BlockSpec((2, x.shape[1], HD), at3) for x in slots]
        + [pl.BlockSpec(memory_space=pl.ANY) for _ in kept],
        out_specs=[pl.BlockSpec((BL, G * HD), at)] + [pl.BlockSpec((2, s[1], HD), at3) for s, _ in shapes[1:]],
        out_shape=[jax.ShapeDtypeStruct(s, d) for s, d in shapes],
        scratch_shapes=[pltpu.VMEM((NS * BL, HD), B16), pltpu.VMEM((NS * BL, HD), B16), pltpu.VMEM((HD, NS * BL), B16)],
        input_output_aliases={n_in + i: i for i in range(len(kept))},
        compiler_params=pltpu.CompilerParams(vmem_limit_bytes=32 << 20),
        cost_estimate=pl.CostEstimate(flops=heads << 30, bytes_accessed=heads << 20, transcendentals=heads << 20),
        name="attention_backward",
    )(mask, q, *grads, *slots, *kept)


def join_body(k, v, out):
    out[0] = k[...]
    out[1] = v[...]


def join(k, v):
    return pl.pallas_call(
        join_body,
        out_shape=jax.ShapeDtypeStruct((2, *k.shape), k.dtype),
        compiler_params=pltpu.CompilerParams(vmem_limit_bytes=4 << 20),
        name="join",
    )(k, v)


def bundle_body(own, left, right, out):
    for i, ref in enumerate((own, left, right)):
        out[:, i * BL : (i + 1) * BL] = ref[...]


def bundle(own, left, right):
    n, rows, cols = own.shape
    return pl.pallas_call(
        bundle_body,
        out_shape=jax.ShapeDtypeStruct((n, 3 * rows, cols), own.dtype),
        compiler_params=pltpu.CompilerParams(vmem_limit_bytes=8 << 20),
        name="bundle",
    )(own, left, right)


def hold_body(*refs):
    pass


def hold(*arrays, flops=1 << 34):
    anywhere = [pl.BlockSpec(memory_space=pl.ANY) for _ in arrays]
    return pl.pallas_call(
        hold_body,
        in_specs=anywhere,
        out_specs=anywhere,
        out_shape=[jax.ShapeDtypeStruct(x.shape, x.dtype) for x in arrays],
        input_output_aliases={i: i for i in range(len(arrays))},
        compiler_params=pltpu.CompilerParams(vmem_limit_bytes=1 << 20),
        cost_estimate=pl.CostEstimate(flops=flops, bytes_accessed=0, transcendentals=0),
        name="hold",
    )(*arrays)


def shift_pairs(count, by):
    return [(i, i + by) for i in range(count) if 0 <= i + by < count]


def mate_pairs(count):
    return [(i, i ^ 1) for i in range(count)]


def far_pairs(count):
    ends = [(i, i + 3 if i % 2 else i - 3) for i in range(count)]
    return [(i, j) for i, j in ends if 0 <= j < count]


def shards(query_heads, key_heads, value_heads, section_cotangent, block_mask):
    sections = lax.axis_size("section")
    count = lax.axis_size("seq")
    half = HQ * HD // 2
    cot = section_cotangent[0]
    before = [(i, (i - 1) % sections) for i in range(sections)]
    own = join(key_heads[0], value_heads[0])
    left, right = hold(
        lax.ppermute(own, "seq", shift_pairs(count, 2)),
        lax.ppermute(own, "seq", shift_pairs(count, -2)),
        flops=1 << 32,
    )
    far, grad_low = hold(
        lax.ppermute(own, "seq", far_pairs(count)),
        lax.ppermute(cot[:, :half], "section", before),
        flops=1 << 33,
    )
    grad_high = lax.ppermute(cot[:, half:], "section", before)
    mate = lax.ppermute(bundle(own, left, right), "seq", mate_pairs(count))
    slots = (own, left, right, far, mate)
    kept = attention_backward(block_mask, query_heads[0], (grad_low,), slots, 0, 2, ())
    query_grad, parts, to_mate, to_far = attention_backward(
        block_mask, query_heads[0], (grad_high,), slots, 2, 2, kept
    )
    (back_far,) = hold(lax.ppermute(to_far, "seq", far_pairs(count)), flops=1 << 33)
    sums = parts + lax.ppermute(to_mate, "seq", mate_pairs(count)).astype(F32)
    back_far, back_left, back_right = hold(
        back_far,
        lax.ppermute(sums[:, BL : 2 * BL].astype(B16), "seq", shift_pairs(count, -2)),
        lax.ppermute(sums[:, 2 * BL :].astype(B16), "seq", shift_pairs(count, 2)),
    )
    total = sums[:, :BL] + back_left.astype(F32) + back_right.astype(F32) + back_far.astype(F32)
    total = total.astype(B16)
    return query_grad[None], total[0][None], total[1][None]


def solution(mesh):
    in_specs = (
        P("section", "seq", None),
        P("section", "seq", None),
        P("section", "seq", None),
        P("section", "seq", None),
        P("seq", None),
    )
    out_specs = (P("section", "seq", None), P("section", "seq", None), P("section", "seq", None))
    return jax.shard_map(shards, mesh=mesh, in_specs=in_specs, out_specs=out_specs, check_vma=False)
```

```python
import functools
import math

import jax
import jax.numpy as jnp
from jax import lax
from jax.experimental import pallas as pl
from jax.experimental.pallas import tpu as pltpu
from jax.sharding import PartitionSpec as P

HQ, HK, HD, W = 32, 4, 128, 3
BL = 128
G = HQ // HK
NS = 2 * W + 1
SCALE = 1.0 / math.sqrt(HD)
LOG2E = math.log2(math.e)
NT = (((1,), (1,)), ((), ()))
NN = (((1,), (0,)), ((), ()))
F32, B16 = jnp.float32, jnp.bfloat16


def slot_offsets(odd):
    sign = 1 - 2 * odd
    return [0, -2, 2, -3 * sign, sign, sign - 2, sign + 2]


def backward_body(n_grads, n_kept, *refs):
    mask, q = refs[:2]
    grads = refs[2 : 2 + n_grads]
    own, left, right, far, mate = refs[2 + n_grads : 7 + n_grads]
    dq, parts, to_mate, to_far, kc, vc, kt = refs[7 + n_grads + n_kept :]
    index = lax.axis_index("seq")
    count = lax.axis_size("seq")
    on = [None]
    for offset in slot_offsets(index % 2)[1:]:
        inside = (index + offset >= 0) & (index + offset < count)
        on.append(inside & (mask[0, offset + W] == 1))
    row = 0
    for ref in (own, left, right, far, mate):
        n = ref.shape[1]
        kc[row : row + n] = ref[0]
        vc[row : row + n] = ref[1]
        row += n
    for s in range(NS):
        kt[:, s * BL : (s + 1) * BL] = kc[s * BL : (s + 1) * BL, :].T
    cols = [slice(i * HD, (i + 1) * HD) for i in range(G)]
    qp = jnp.concatenate([q[:, c] for c in cols], axis=0)
    gp = jnp.concatenate([grads[0][:, c] for c in cols], axis=0)
    for more in grads[1:]:
        gp = gp + jnp.concatenate([more[:, c] for c in cols], axis=0)
    s = lax.dot_general(kc[...], qp, NT, preferred_element_type=F32)
    pieces = [s[i * BL : (i + 1) * BL] for i in range(NS)]
    pieces = [p if f is None else jnp.where(f, p, -jnp.inf) for p, f in zip(pieces, on)]
    s = jnp.concatenate(pieces, axis=0)
    m = jnp.max(s, axis=0, keepdims=True)
    e = jnp.exp2((s - m) * (SCALE * LOG2E))
    p = e * (1.0 / jnp.sum(e, axis=0, keepdims=True))
    dp = lax.dot_general(vc[...], gp, NT, preferred_element_type=F32)
    delta = jnp.sum(p * dp, axis=0, keepdims=True)
    ds = (p * (dp - delta)).astype(B16)
    dv = lax.dot_general(p.astype(B16), gp, NN, preferred_element_type=F32)
    dk = lax.dot_general(ds, qp, NN, preferred_element_type=F32) * SCALE
    dqt = lax.dot_general(kt[...], ds, NN, preferred_element_type=F32)
    for i, c in enumerate(cols):
        dq[:, c] = (dqt[:, c].T * SCALE).astype(B16)
    for i, d in enumerate((dk, dv)):
        parts[i] = d[: 3 * BL]
        to_far[i] = d[3 * BL : 4 * BL].astype(B16)
        to_mate[i] = d[4 * BL :].astype(B16)


def attention_backward(mask, q, grads, slots, first, heads, kept):
    at = lambda h: (0, h + first)
    at3 = lambda h: (0, 0, h + first)
    here = lambda h: (0, h)
    width = HK * HD
    shapes = [((BL, HQ * HD), B16), ((2, 3 * BL, width), F32), ((2, 3 * BL, width), B16), ((2, BL, width), B16)]
    n_in = 2 + len(grads) + len(slots)
    return pl.pallas_call(
        functools.partial(backward_body, len(grads), len(kept)),
        grid=(heads,),
        in_specs=[pl.BlockSpec(memory_space=pltpu.SMEM), pl.BlockSpec((BL, G * HD), at)]
        + [pl.BlockSpec((BL, G * HD), here) for _ in grads]
        + [pl.BlockSpec((2, x.shape[1], HD), at3) for x in slots]
        + [pl.BlockSpec(memory_space=pl.ANY) for _ in kept],
        out_specs=[pl.BlockSpec((BL, G * HD), at)] + [pl.BlockSpec((2, s[1], HD), at3) for s, _ in shapes[1:]],
        out_shape=[jax.ShapeDtypeStruct(s, d) for s, d in shapes],
        scratch_shapes=[pltpu.VMEM((NS * BL, HD), B16), pltpu.VMEM((NS * BL, HD), B16), pltpu.VMEM((HD, NS * BL), B16)],
        input_output_aliases={n_in + i: i for i in range(len(kept))},
        compiler_params=pltpu.CompilerParams(vmem_limit_bytes=32 << 20),
        cost_estimate=pl.CostEstimate(flops=heads << 30, bytes_accessed=heads << 20, transcendentals=heads << 20),
        name="attention_backward",
    )(mask, q, *grads, *slots, *kept)


def join_body(k, v, out):
    out[0] = k[...]
    out[1] = v[...]


def join(k, v):
    return pl.pallas_call(
        join_body,
        out_shape=jax.ShapeDtypeStruct((2, *k.shape), k.dtype),
        compiler_params=pltpu.CompilerParams(vmem_limit_bytes=4 << 20),
        name="join",
    )(k, v)


def bundle_body(own, left, right, out):
    for i, ref in enumerate((own, left, right)):
        out[:, i * BL : (i + 1) * BL] = ref[...]


def bundle(own, left, right):
    n, rows, cols = own.shape
    return pl.pallas_call(
        bundle_body,
        out_shape=jax.ShapeDtypeStruct((n, 3 * rows, cols), own.dtype),
        compiler_params=pltpu.CompilerParams(vmem_limit_bytes=8 << 20),
        name="bundle",
    )(own, left, right)


def hold_body(*refs):
    pass


def hold(*arrays, flops=1 << 34):
    anywhere = [pl.BlockSpec(memory_space=pl.ANY) for _ in arrays]
    return pl.pallas_call(
        hold_body,
        in_specs=anywhere,
        out_specs=anywhere,
        out_shape=[jax.ShapeDtypeStruct(x.shape, x.dtype) for x in arrays],
        input_output_aliases={i: i for i in range(len(arrays))},
        compiler_params=pltpu.CompilerParams(vmem_limit_bytes=1 << 20),
        cost_estimate=pl.CostEstimate(flops=flops, bytes_accessed=0, transcendentals=0),
        name="hold",
    )(*arrays)


def shift_pairs(count, by):
    return [(i, i + by) for i in range(count) if 0 <= i + by < count]


def mate_pairs(count):
    return [(i, i ^ 1) for i in range(count)]


def far_pairs(count):
    ends = [(i, i + 3 if i % 2 else i - 3) for i in range(count)]
    return [(i, j) for i, j in ends if 0 <= j < count]


def shards(query_heads, key_heads, value_heads, section_cotangent, block_mask):
    sections = lax.axis_size("section")
    count = lax.axis_size("seq")
    half = HQ * HD // 2
    turn = sections // 2
    cot = section_cotangent[0]
    low, high = cot[:, :half], cot[:, half:]
    before = [(i, (i - 1) % sections) for i in range(sections)]
    own = join(key_heads[0], value_heads[0])
    left, right = hold(
        lax.ppermute(own, "seq", shift_pairs(count, 2)),
        lax.ppermute(own, "seq", shift_pairs(count, -2)),
        flops=1 << 32,
    )
    far, grad_low = hold(
        lax.ppermute(own, "seq", far_pairs(count)), lax.ppermute(low, "section", before), flops=1 << 33
    )
    (turned,) = hold(lax.ppermute(high, "section", [(0, turn), (turn, 0)]), flops=1 << 33)
    joined, high = lax.optimization_barrier((bundle(own, left, right), high))
    mate = lax.ppermute(joined, "seq", mate_pairs(count))
    grad_high = lax.ppermute(high, "section", [(i, i - 1) for i in range(sections) if i % turn])
    grad_wrap = lax.ppermute(turned, "section", [(0, turn - 1), (turn, sections - 1)])
    slots = (own, left, right, far, mate)
    kept = attention_backward(block_mask, query_heads[0], (grad_low,), slots, 0, 2, ())
    query_grad, parts, to_mate, to_far = attention_backward(
        block_mask, query_heads[0], (grad_high, grad_wrap), slots, 2, 2, kept
    )
    (back_far,) = hold(lax.ppermute(to_far, "seq", far_pairs(count)), flops=1 << 33)
    sums = parts + lax.ppermute(to_mate, "seq", mate_pairs(count)).astype(F32)
    back_far, back_left, back_right = hold(
        back_far,
        lax.ppermute(sums[:, BL : 2 * BL].astype(B16), "seq", shift_pairs(count, -2)),
        lax.ppermute(sums[:, 2 * BL :].astype(B16), "seq", shift_pairs(count, 2)),
    )
    total = sums[:, :BL] + back_left.astype(F32) + back_right.astype(F32) + back_far.astype(F32)
    total = total.astype(B16)
    return query_grad[None], total[0][None], total[1][None]


def solution(mesh):
    in_specs = (
        P("section", "seq", None),
        P("section", "seq", None),
        P("section", "seq", None),
        P("section", "seq", None),
        P("seq", None),
    )
    out_specs = (P("section", "seq", None), P("section", "seq", None), P("section", "seq", None))
    return jax.shard_map(shards, mesh=mesh, in_specs=in_specs, out_specs=out_specs, check_vma=False)
```

```python
import functools
import math

import jax
import jax.numpy as jnp
from jax import lax
from jax.experimental import pallas as pl
from jax.experimental.pallas import tpu as pltpu
from jax.sharding import PartitionSpec as P

HQ, HK, HD, W = 32, 4, 128, 3
BL = 128
COLUMNS = 4
G = HQ // HK
NS = 2 * W + 1
SCALE = 1.0 / math.sqrt(HD)
LOG2E = math.log2(math.e)
NT = (((1,), (1,)), ((), ()))
NN = (((1,), (0,)), ((), ()))
F32, B16 = jnp.float32, jnp.bfloat16


def slot_offsets(odd):
    sign = 1 - 2 * odd
    return [0, -2, 2, -3 * sign, sign, sign - 2, sign + 2]


def backward_body(n_grads, n_kept, *refs):
    mask, q = refs[:2]
    grads = refs[2 : 2 + n_grads]
    own, left, right, far, mate = refs[2 + n_grads : 7 + n_grads]
    dq, parts, to_mate, to_far, kc, vc, kt = refs[7 + n_grads + n_kept :]
    index = lax.axis_index("seq")
    count = lax.axis_size("seq")
    on = [None]
    for offset in slot_offsets(index % 2)[1:]:
        inside = (index + offset >= 0) & (index + offset < count)
        on.append(inside & (mask[0, offset + W] == 1))
    row = 0
    for ref in (own, left, right, far, mate):
        n = ref.shape[1]
        kc[row : row + n] = ref[0]
        vc[row : row + n] = ref[1]
        row += n
    for s in range(NS):
        kt[:, s * BL : (s + 1) * BL] = kc[s * BL : (s + 1) * BL, :].T
    cols = [slice(i * HD, (i + 1) * HD) for i in range(G)]
    qp = jnp.concatenate([q[:, c] for c in cols], axis=0)
    gp = jnp.concatenate([grads[0][:, c] for c in cols], axis=0)
    for more in grads[1:]:
        gp = gp + jnp.concatenate([more[:, c] for c in cols], axis=0)
    s = lax.dot_general(kc[...], qp, NT, preferred_element_type=F32)
    pieces = [s[i * BL : (i + 1) * BL] for i in range(NS)]
    pieces = [p if f is None else jnp.where(f, p, -jnp.inf) for p, f in zip(pieces, on)]
    s = jnp.concatenate(pieces, axis=0)
    m = jnp.max(s, axis=0, keepdims=True)
    e = jnp.exp2((s - m) * (SCALE * LOG2E))
    p = e * (1.0 / jnp.sum(e, axis=0, keepdims=True))
    dp = lax.dot_general(vc[...], gp, NT, preferred_element_type=F32)
    delta = jnp.sum(p * dp, axis=0, keepdims=True)
    ds = (p * (dp - delta)).astype(B16)
    dv = lax.dot_general(p.astype(B16), gp, NN, preferred_element_type=F32)
    dk = lax.dot_general(ds, qp, NN, preferred_element_type=F32) * SCALE
    dqt = lax.dot_general(kt[...], ds, NN, preferred_element_type=F32)
    for i, c in enumerate(cols):
        dq[:, c] = (dqt[:, c].T * SCALE).astype(B16)
    for i, d in enumerate((dk, dv)):
        parts[i] = d[: 3 * BL]
        to_far[i] = d[3 * BL : 4 * BL].astype(B16)
        to_mate[i] = d[4 * BL :].astype(B16)


def attention_backward(mask, q, grads, slots, first, heads, kept):
    at = lambda h: (0, h + first)
    at3 = lambda h: (0, 0, h + first)
    here = lambda h: (0, h)
    width = HK * HD
    shapes = [((BL, HQ * HD), B16), ((2, 3 * BL, width), F32), ((2, 3 * BL, width), B16), ((2, BL, width), B16)]
    n_in = 2 + len(grads) + len(slots)
    return pl.pallas_call(
        functools.partial(backward_body, len(grads), len(kept)),
        grid=(heads,),
        in_specs=[pl.BlockSpec(memory_space=pltpu.SMEM), pl.BlockSpec((BL, G * HD), at)]
        + [pl.BlockSpec((BL, G * HD), here) for _ in grads]
        + [pl.BlockSpec((2, x.shape[1], HD), at3) for x in slots]
        + [pl.BlockSpec(memory_space=pl.ANY) for _ in kept],
        out_specs=[pl.BlockSpec((BL, G * HD), at)] + [pl.BlockSpec((2, s[1], HD), at3) for s, _ in shapes[1:]],
        out_shape=[jax.ShapeDtypeStruct(s, d) for s, d in shapes],
        scratch_shapes=[pltpu.VMEM((NS * BL, HD), B16), pltpu.VMEM((NS * BL, HD), B16), pltpu.VMEM((HD, NS * BL), B16)],
        input_output_aliases={n_in + i: i for i in range(len(kept))},
        compiler_params=pltpu.CompilerParams(vmem_limit_bytes=32 << 20),
        cost_estimate=pl.CostEstimate(flops=heads << 30, bytes_accessed=heads << 20, transcendentals=heads << 20),
        name="attention_backward",
    )(mask, q, *grads, *slots, *kept)


def join_body(k, v, out):
    out[0] = k[...]
    out[1] = v[...]


def join(k, v):
    return pl.pallas_call(
        join_body,
        out_shape=jax.ShapeDtypeStruct((2, *k.shape), k.dtype),
        compiler_params=pltpu.CompilerParams(vmem_limit_bytes=4 << 20),
        name="join",
    )(k, v)


def bundle_body(own, left, right, out):
    for i, ref in enumerate((own, left, right)):
        out[:, i * BL : (i + 1) * BL] = ref[...]


def bundle(own, left, right):
    n, rows, cols = own.shape
    return pl.pallas_call(
        bundle_body,
        out_shape=jax.ShapeDtypeStruct((n, 3 * rows, cols), own.dtype),
        compiler_params=pltpu.CompilerParams(vmem_limit_bytes=8 << 20),
        name="bundle",
    )(own, left, right)


def hold_body(*refs):
    pass


def hold(*arrays, flops=1 << 34):
    anywhere = [pl.BlockSpec(memory_space=pl.ANY) for _ in arrays]
    return pl.pallas_call(
        hold_body,
        in_specs=anywhere,
        out_specs=anywhere,
        out_shape=[jax.ShapeDtypeStruct(x.shape, x.dtype) for x in arrays],
        input_output_aliases={i: i for i in range(len(arrays))},
        compiler_params=pltpu.CompilerParams(vmem_limit_bytes=1 << 20),
        cost_estimate=pl.CostEstimate(flops=flops, bytes_accessed=0, transcendentals=0),
        name="hold",
    )(*arrays)


def shift_pairs(count, by):
    return [(i, i + by) for i in range(count) if 0 <= i + by < count]


def mate_pairs(count):
    return [(i, i ^ 1) for i in range(count)]


def far_pairs(count):
    ends = [(i, i + 3 if i % 2 else i - 3) for i in range(count)]
    return [(i, j) for i, j in ends if 0 <= j < count]


def wrap_routes(sections, count):
    straight, turning, wrapping = [], [], []
    for i in range(sections):
        for j in range(count):
            here, there = i * count + j, (i - 1) % sections * count + j
            column = j // 2 % COLUMNS
            if i % (sections // 2) or column not in (0, COLUMNS - 1):
                straight.append((here, there))
            else:
                via = (i + sections // 2) % sections * count + j + (2 if column == 0 else -2)
                turning.append((here, via))
                wrapping.append((via, there))
    return straight, turning, wrapping


def shards(query_heads, key_heads, value_heads, section_cotangent, block_mask):
    sections = lax.axis_size("section")
    count = lax.axis_size("seq")
    half = HQ * HD // 2
    cot = section_cotangent[0]
    low, high = cot[:, :half], cot[:, half:]
    straight, turning, wrapping = wrap_routes(sections, count)
    before = [(i, (i - 1) % sections) for i in range(sections)]
    both = ("section", "seq")
    own = join(key_heads[0], value_heads[0])
    left, right = hold(
        lax.ppermute(own, "seq", shift_pairs(count, 2)),
        lax.ppermute(own, "seq", shift_pairs(count, -2)),
        flops=1 << 32,
    )
    far, grad_low = hold(
        lax.ppermute(own, "seq", far_pairs(count)), lax.ppermute(low, both, straight), flops=1 << 33
    )
    (turned,) = hold(lax.ppermute(low, both, turning), flops=1 << 33)
    joined, high = lax.optimization_barrier((bundle(own, left, right), high))
    mate = lax.ppermute(joined, "seq", mate_pairs(count))
    grad_high = lax.ppermute(high, "section", before)
    grad_wrap = lax.ppermute(turned, both, wrapping)
    slots = (own, left, right, far, mate)
    kept = attention_backward(block_mask, query_heads[0], (grad_low, grad_wrap), slots, 0, 2, ())
    query_grad, parts, to_mate, to_far = attention_backward(
        block_mask, query_heads[0], (grad_high,), slots, 2, 2, kept
    )
    (back_far,) = hold(lax.ppermute(to_far, "seq", far_pairs(count)), flops=1 << 33)
    sums = parts + lax.ppermute(to_mate, "seq", mate_pairs(count)).astype(F32)
    back_far, back_left, back_right = hold(
        back_far,
        lax.ppermute(sums[:, BL : 2 * BL].astype(B16), "seq", shift_pairs(count, -2)),
        lax.ppermute(sums[:, 2 * BL :].astype(B16), "seq", shift_pairs(count, 2)),
    )
    total = sums[:, :BL] + back_left.astype(F32) + back_right.astype(F32) + back_far.astype(F32)
    total = total.astype(B16)
    return query_grad[None], total[0][None], total[1][None]


def solution(mesh):
    in_specs = (
        P("section", "seq", None),
        P("section", "seq", None),
        P("section", "seq", None),
        P("section", "seq", None),
        P("seq", None),
    )
    out_specs = (P("section", "seq", None), P("section", "seq", None), P("section", "seq", None))
    return jax.shard_map(shards, mesh=mesh, in_specs=in_specs, out_specs=out_specs, check_vma=False)
```

```python
import functools
import math

import jax
import jax.numpy as jnp
from jax import lax
from jax.experimental import pallas as pl
from jax.experimental.pallas import tpu as pltpu
from jax.sharding import PartitionSpec as P

HQ, HK, HD, W = 32, 4, 128, 3
BL = 128
COLUMNS = 4
G = HQ // HK
NS = 2 * W + 1
SCALE = 1.0 / math.sqrt(HD)
LOG2E = math.log2(math.e)
NT = (((1,), (1,)), ((), ()))
NN = (((1,), (0,)), ((), ()))
F32, B16 = jnp.float32, jnp.bfloat16


def slot_offsets(odd):
    sign = 1 - 2 * odd
    return [0, -2, 2, -3 * sign, sign, sign - 2, sign + 2]


def backward_body(n_grads, n_kept, *refs):
    mask, q = refs[:2]
    grads = refs[2 : 2 + n_grads]
    own, left, right, far, mate = refs[2 + n_grads : 7 + n_grads]
    dq, parts, to_mate, to_far, kc, vc, kt = refs[7 + n_grads + n_kept :]
    index = lax.axis_index("seq")
    count = lax.axis_size("seq")
    on = [None]
    for offset in slot_offsets(index % 2)[1:]:
        inside = (index + offset >= 0) & (index + offset < count)
        on.append(inside & (mask[0, offset + W] == 1))
    row = 0
    for ref in (own, left, right, far, mate):
        n = ref.shape[1]
        kc[row : row + n] = ref[0]
        vc[row : row + n] = ref[1]
        row += n
    for s in range(NS):
        kt[:, s * BL : (s + 1) * BL] = kc[s * BL : (s + 1) * BL, :].T
    cols = [slice(i * HD, (i + 1) * HD) for i in range(G)]
    qp = jnp.concatenate([q[:, c] for c in cols], axis=0)
    gp = jnp.concatenate([grads[0][:, c] for c in cols], axis=0)
    for more in grads[1:]:
        gp = gp + jnp.concatenate([more[:, c] for c in cols], axis=0)
    s = lax.dot_general(kc[...], qp, NT, preferred_element_type=F32)
    pieces = [s[i * BL : (i + 1) * BL] for i in range(NS)]
    pieces = [p if f is None else jnp.where(f, p, -jnp.inf) for p, f in zip(pieces, on)]
    s = jnp.concatenate(pieces, axis=0)
    m = jnp.max(s, axis=0, keepdims=True)
    e = jnp.exp2((s - m) * (SCALE * LOG2E))
    p = e * (1.0 / jnp.sum(e, axis=0, keepdims=True))
    dp = lax.dot_general(vc[...], gp, NT, preferred_element_type=F32)
    delta = jnp.sum(p * dp, axis=0, keepdims=True)
    ds = (p * (dp - delta)).astype(B16)
    dv = lax.dot_general(p.astype(B16), gp, NN, preferred_element_type=F32)
    dk = lax.dot_general(ds, qp, NN, preferred_element_type=F32) * SCALE
    dqt = lax.dot_general(kt[...], ds, NN, preferred_element_type=F32)
    for i, c in enumerate(cols):
        dq[:, c] = (dqt[:, c].T * SCALE).astype(B16)
    for i, d in enumerate((dk, dv)):
        parts[i] = d[: 3 * BL]
        to_far[i] = d[3 * BL : 4 * BL].astype(B16)
        to_mate[i] = d[4 * BL :].astype(B16)


def attention_backward(mask, q, grads, slots, first, heads, kept):
    at = lambda h: (0, h + first)
    at3 = lambda h: (0, 0, h + first)
    here = lambda h: (0, h)
    width = HK * HD
    shapes = [((BL, HQ * HD), B16), ((2, 3 * BL, width), F32), ((2, 3 * BL, width), B16), ((2, BL, width), B16)]
    n_in = 2 + len(grads) + len(slots)
    return pl.pallas_call(
        functools.partial(backward_body, len(grads), len(kept)),
        grid=(heads,),
        in_specs=[pl.BlockSpec(memory_space=pltpu.SMEM), pl.BlockSpec((BL, G * HD), at)]
        + [pl.BlockSpec((BL, G * HD), here) for _ in grads]
        + [pl.BlockSpec((2, x.shape[1], HD), at3) for x in slots]
        + [pl.BlockSpec(memory_space=pl.ANY) for _ in kept],
        out_specs=[pl.BlockSpec((BL, G * HD), at)] + [pl.BlockSpec((2, s[1], HD), at3) for s, _ in shapes[1:]],
        out_shape=[jax.ShapeDtypeStruct(s, d) for s, d in shapes],
        scratch_shapes=[pltpu.VMEM((NS * BL, HD), B16), pltpu.VMEM((NS * BL, HD), B16), pltpu.VMEM((HD, NS * BL), B16)],
        input_output_aliases={n_in + i: i for i in range(len(kept))},
        compiler_params=pltpu.CompilerParams(vmem_limit_bytes=32 << 20),
        cost_estimate=pl.CostEstimate(flops=heads << 30, bytes_accessed=heads << 20, transcendentals=heads << 20),
        name="attention_backward",
    )(mask, q, *grads, *slots, *kept)


def join_body(k, v, out):
    out[0] = k[...]
    out[1] = v[...]


def join(k, v):
    return pl.pallas_call(
        join_body,
        out_shape=jax.ShapeDtypeStruct((2, *k.shape), k.dtype),
        compiler_params=pltpu.CompilerParams(vmem_limit_bytes=4 << 20),
        name="join",
    )(k, v)


def bundle_body(own, left, right, out):
    for i, ref in enumerate((own, left, right)):
        out[:, i * BL : (i + 1) * BL] = ref[...]


def bundle(own, left, right):
    n, rows, cols = own.shape
    return pl.pallas_call(
        bundle_body,
        out_shape=jax.ShapeDtypeStruct((n, 3 * rows, cols), own.dtype),
        compiler_params=pltpu.CompilerParams(vmem_limit_bytes=8 << 20),
        name="bundle",
    )(own, left, right)


def hold_body(*refs):
    pass


def hold(*arrays, flops=1 << 34):
    anywhere = [pl.BlockSpec(memory_space=pl.ANY) for _ in arrays]
    return pl.pallas_call(
        hold_body,
        in_specs=anywhere,
        out_specs=anywhere,
        out_shape=[jax.ShapeDtypeStruct(x.shape, x.dtype) for x in arrays],
        input_output_aliases={i: i for i in range(len(arrays))},
        compiler_params=pltpu.CompilerParams(vmem_limit_bytes=1 << 20),
        cost_estimate=pl.CostEstimate(flops=flops, bytes_accessed=0, transcendentals=0),
        name="hold",
    )(*arrays)


def shift_pairs(count, by):
    return [(i, i + by) for i in range(count) if 0 <= i + by < count]


def mate_pairs(count):
    return [(i, i ^ 1) for i in range(count)]


def far_pairs(count):
    ends = [(i, i + 3 if i % 2 else i - 3) for i in range(count)]
    return [(i, j) for i, j in ends if 0 <= j < count]


def wrap_routes(sections, count):
    straight, turning, wrapping = [], [], []
    for i in range(sections):
        for j in range(count):
            here, there = i * count + j, (i - 1) % sections * count + j
            column = j // 2 % COLUMNS
            if i % (sections // 2) or column not in (0, COLUMNS - 1):
                straight.append((here, there))
            else:
                via = (i + sections // 2) % sections * count + j + (2 if column == 0 else -2)
                turning.append((here, via))
                wrapping.append((via, there))
    return straight, turning, wrapping


def shards(query_heads, key_heads, value_heads, section_cotangent, block_mask):
    sections = lax.axis_size("section")
    count = lax.axis_size("seq")
    half = HQ * HD // 2
    cot = section_cotangent[0]
    low, high = cot[:, :half], cot[:, half:]
    straight, turning, wrapping = wrap_routes(sections, count)
    before = [(i, (i - 1) % sections) for i in range(sections)]
    both = ("section", "seq")
    own = join(key_heads[0], value_heads[0])
    left, right = hold(
        lax.ppermute(own, "seq", shift_pairs(count, 2)),
        lax.ppermute(own, "seq", shift_pairs(count, -2)),
        flops=1 << 32,
    )
    far, grad_low = hold(
        lax.ppermute(own, "seq", far_pairs(count)), lax.ppermute(low, "section", before), flops=1 << 33
    )
    (turned,) = hold(lax.ppermute(high, both, turning), flops=1 << 33)
    joined, late = lax.optimization_barrier((bundle(own, left, right), high))
    mate = lax.ppermute(joined, "seq", mate_pairs(count))
    grad_high = lax.ppermute(late, both, straight)
    grad_wrap = lax.ppermute(turned, both, wrapping)
    slots = (own, left, right, far, mate)
    kept = attention_backward(block_mask, query_heads[0], (grad_low,), slots, 0, 2, ())
    query_grad, parts, to_mate, to_far = attention_backward(
        block_mask, query_heads[0], (grad_high, grad_wrap), slots, 2, 2, kept
    )
    (back_far,) = hold(lax.ppermute(to_far, "seq", far_pairs(count)), flops=1 << 33)
    sums = parts + lax.ppermute(to_mate, "seq", mate_pairs(count)).astype(F32)
    back_far, back_left, back_right = hold(
        back_far,
        lax.ppermute(sums[:, BL : 2 * BL].astype(B16), "seq", shift_pairs(count, -2)),
        lax.ppermute(sums[:, 2 * BL :].astype(B16), "seq", shift_pairs(count, 2)),
    )
    total = sums[:, :BL] + back_left.astype(F32) + back_right.astype(F32) + back_far.astype(F32)
    total = total.astype(B16)
    return query_grad[None], total[0][None], total[1][None]


def solution(mesh):
    in_specs = (
        P("section", "seq", None),
        P("section", "seq", None),
        P("section", "seq", None),
        P("section", "seq", None),
        P("seq", None),
    )
    out_specs = (P("section", "seq", None), P("section", "seq", None), P("section", "seq", None))
    return jax.shard_map(shards, mesh=mesh, in_specs=in_specs, out_specs=out_specs, check_vma=False)
```

```python
import functools
import math

import jax
import jax.numpy as jnp
from jax import lax
from jax.experimental import pallas as pl
from jax.experimental.pallas import tpu as pltpu
from jax.sharding import PartitionSpec as P

HQ, HK, HD, W = 32, 4, 128, 3
BL = 128
G = HQ // HK
NS = 2 * W + 1
SCALE = 1.0 / math.sqrt(HD)
LOG2E = math.log2(math.e)
NT = (((1,), (1,)), ((), ()))
NN = (((1,), (0,)), ((), ()))
F32, B16 = jnp.float32, jnp.bfloat16


def slot_offsets(odd):
    sign = 1 - 2 * odd
    return [0, -2, 2, -3 * sign, sign, sign - 2, sign + 2]


def backward_body(n_grads, n_kept, *refs):
    mask, q = refs[:2]
    grads = refs[2 : 2 + n_grads]
    own, left, right, far, mate = refs[2 + n_grads : 7 + n_grads]
    dq, parts, to_mate, to_far, kc, vc, kt = refs[7 + n_grads + n_kept :]
    index = lax.axis_index("seq")
    count = lax.axis_size("seq")
    on = [None]
    for offset in slot_offsets(index % 2)[1:]:
        inside = (index + offset >= 0) & (index + offset < count)
        on.append(inside & (mask[0, offset + W] == 1))
    row = 0
    for ref in (own, left, right, far, mate):
        n = ref.shape[1]
        kc[row : row + n] = ref[0]
        vc[row : row + n] = ref[1]
        row += n
    for s in range(NS):
        kt[:, s * BL : (s + 1) * BL] = kc[s * BL : (s + 1) * BL, :].T
    cols = [slice(i * HD, (i + 1) * HD) for i in range(G)]
    qp = jnp.concatenate([q[:, c] for c in cols], axis=0)
    gp = jnp.concatenate([grads[0][:, c] for c in cols], axis=0)
    for more in grads[1:]:
        gp = gp + jnp.concatenate([more[:, c] for c in cols], axis=0)
    s = lax.dot_general(kc[...], qp, NT, preferred_element_type=F32)
    pieces = [s[i * BL : (i + 1) * BL] for i in range(NS)]
    pieces = [p if f is None else jnp.where(f, p, -jnp.inf) for p, f in zip(pieces, on)]
    s = jnp.concatenate(pieces, axis=0)
    m = jnp.max(s, axis=0, keepdims=True)
    e = jnp.exp2((s - m) * (SCALE * LOG2E))
    p = e * (1.0 / jnp.sum(e, axis=0, keepdims=True))
    dp = lax.dot_general(vc[...], gp, NT, preferred_element_type=F32)
    delta = jnp.sum(p * dp, axis=0, keepdims=True)
    ds = (p * (dp - delta)).astype(B16)
    dv = lax.dot_general(p.astype(B16), gp, NN, preferred_element_type=F32)
    dk = lax.dot_general(ds, qp, NN, preferred_element_type=F32) * SCALE
    dqt = lax.dot_general(kt[...], ds, NN, preferred_element_type=F32)
    for i, c in enumerate(cols):
        dq[:, c] = (dqt[:, c].T * SCALE).astype(B16)
    for i, d in enumerate((dk, dv)):
        parts[i] = d[: 3 * BL]
        to_far[i] = d[3 * BL : 4 * BL].astype(B16)
        to_mate[i] = d[4 * BL :].astype(B16)


def attention_backward(mask, q, grads, slots, first, heads, kept):
    at = lambda h: (0, h + first)
    at3 = lambda h: (0, 0, h + first)
    here = lambda h: (0, h)
    width = HK * HD
    shapes = [((BL, HQ * HD), B16), ((2, 3 * BL, width), F32), ((2, 3 * BL, width), B16), ((2, BL, width), B16)]
    n_in = 2 + len(grads) + len(slots)
    return pl.pallas_call(
        functools.partial(backward_body, len(grads), len(kept)),
        grid=(heads,),
        in_specs=[pl.BlockSpec(memory_space=pltpu.SMEM), pl.BlockSpec((BL, G * HD), at)]
        + [pl.BlockSpec((BL, G * HD), here) for _ in grads]
        + [pl.BlockSpec((2, x.shape[1], HD), at3) for x in slots]
        + [pl.BlockSpec(memory_space=pl.ANY) for _ in kept],
        out_specs=[pl.BlockSpec((BL, G * HD), at)] + [pl.BlockSpec((2, s[1], HD), at3) for s, _ in shapes[1:]],
        out_shape=[jax.ShapeDtypeStruct(s, d) for s, d in shapes],
        scratch_shapes=[pltpu.VMEM((NS * BL, HD), B16), pltpu.VMEM((NS * BL, HD), B16), pltpu.VMEM((HD, NS * BL), B16)],
        input_output_aliases={n_in + i: i for i in range(len(kept))},
        compiler_params=pltpu.CompilerParams(vmem_limit_bytes=32 << 20),
        cost_estimate=pl.CostEstimate(flops=heads << 30, bytes_accessed=heads << 20, transcendentals=heads << 20),
        name="attention_backward",
    )(mask, q, *grads, *slots, *kept)


def join_body(k, v, out):
    out[0] = k[...]
    out[1] = v[...]


def join(k, v):
    return pl.pallas_call(
        join_body,
        out_shape=jax.ShapeDtypeStruct((2, *k.shape), k.dtype),
        compiler_params=pltpu.CompilerParams(vmem_limit_bytes=4 << 20),
        name="join",
    )(k, v)


def bundle_body(own, left, right, out):
    for i, ref in enumerate((own, left, right)):
        out[:, i * BL : (i + 1) * BL] = ref[...]


def bundle(own, left, right):
    n, rows, cols = own.shape
    return pl.pallas_call(
        bundle_body,
        out_shape=jax.ShapeDtypeStruct((n, 3 * rows, cols), own.dtype),
        compiler_params=pltpu.CompilerParams(vmem_limit_bytes=8 << 20),
        name="bundle",
    )(own, left, right)


def hold_body(*refs):
    pass


def hold(*arrays, flops=1 << 34):
    anywhere = [pl.BlockSpec(memory_space=pl.ANY) for _ in arrays]
    return pl.pallas_call(
        hold_body,
        in_specs=anywhere,
        out_specs=anywhere,
        out_shape=[jax.ShapeDtypeStruct(x.shape, x.dtype) for x in arrays],
        input_output_aliases={i: i for i in range(len(arrays))},
        compiler_params=pltpu.CompilerParams(vmem_limit_bytes=1 << 20),
        cost_estimate=pl.CostEstimate(flops=flops, bytes_accessed=0, transcendentals=0),
        name="hold",
    )(*arrays)


def shift_pairs(count, by):
    return [(i, i + by) for i in range(count) if 0 <= i + by < count]


def mate_pairs(count):
    return [(i, i ^ 1) for i in range(count)]


def far_pairs(count):
    ends = [(i, i + 3 if i % 2 else i - 3) for i in range(count)]
    return [(i, j) for i, j in ends if 0 <= j < count]


def shards(query_heads, key_heads, value_heads, section_cotangent, block_mask):
    sections = lax.axis_size("section")
    count = lax.axis_size("seq")
    half = HQ * HD // 2
    turn = sections // 2
    cot = section_cotangent[0]
    low, high = cot[:, :half], cot[:, half:]
    before = [(i, (i - 1) % sections) for i in range(sections)]
    own = join(key_heads[0], value_heads[0])
    left, right = hold(
        lax.ppermute(own, "seq", shift_pairs(count, 2)),
        lax.ppermute(own, "seq", shift_pairs(count, -2)),
        flops=1 << 32,
    )
    far, grad_low = hold(
        lax.ppermute(own, "seq", far_pairs(count)), lax.ppermute(low, "section", before), flops=1 << 33
    )
    (turned,) = hold(lax.ppermute(high, "section", [(0, turn), (turn, 0)]), flops=1 << 33)
    left, right, late = lax.optimization_barrier((left, right, high))
    left, right, turned = lax.optimization_barrier((left, right, turned))
    mate = lax.ppermute(bundle(own, left, right), "seq", mate_pairs(count))
    grad_high = lax.ppermute(late, "section", [(i, i - 1) for i in range(sections) if i % turn])
    grad_wrap = lax.ppermute(turned, "section", [(0, turn - 1), (turn, sections - 1)])
    slots = (own, left, right, far, mate)
    kept = attention_backward(block_mask, query_heads[0], (grad_low,), slots, 0, 2, ())
    grad_wrap, last = hold(grad_wrap, kept[3], flops=1 << 31)
    kept = [*kept[:3], last]
    query_grad, parts, to_mate, to_far = attention_backward(
        block_mask, query_heads[0], (grad_high, grad_wrap), slots, 2, 2, kept
    )
    (back_far,) = hold(lax.ppermute(to_far, "seq", far_pairs(count)), flops=1 << 33)
    sums = parts + lax.ppermute(to_mate, "seq", mate_pairs(count)).astype(F32)
    back_far, back_left, back_right = hold(
        back_far,
        lax.ppermute(sums[:, BL : 2 * BL].astype(B16), "seq", shift_pairs(count, -2)),
        lax.ppermute(sums[:, 2 * BL :].astype(B16), "seq", shift_pairs(count, 2)),
    )
    total = sums[:, :BL] + back_left.astype(F32) + back_right.astype(F32) + back_far.astype(F32)
    total = total.astype(B16)
    return query_grad[None], total[0][None], total[1][None]


def solution(mesh):
    in_specs = (
        P("section", "seq", None),
        P("section", "seq", None),
        P("section", "seq", None),
        P("section", "seq", None),
        P("seq", None),
    )
    out_specs = (P("section", "seq", None), P("section", "seq", None), P("section", "seq", None))
    return jax.shard_map(shards, mesh=mesh, in_specs=in_specs, out_specs=out_specs, check_vma=False)
```

```python
import functools
import math

import jax
import jax.numpy as jnp
from jax import lax
from jax.experimental import pallas as pl
from jax.experimental.pallas import tpu as pltpu
from jax.sharding import PartitionSpec as P

HQ, HK, HD, W = 32, 4, 128, 3
BL = 128
G = HQ // HK
NS = 2 * W + 1
SCALE = 1.0 / math.sqrt(HD)
LOG2E = math.log2(math.e)
NT = (((1,), (1,)), ((), ()))
NN = (((1,), (0,)), ((), ()))
F32, B16 = jnp.float32, jnp.bfloat16


def slot_offsets(odd):
    sign = 1 - 2 * odd
    return [0, -2, 2, -3 * sign, sign, sign - 2, sign + 2]


def backward_body(n_grads, n_kept, *refs):
    mask, q = refs[:2]
    grads = refs[2 : 2 + n_grads]
    own, left, right, far, mate = refs[2 + n_grads : 7 + n_grads]
    dq, parts, to_mate, to_far, kc, vc, kt = refs[7 + n_grads + n_kept :]
    index = lax.axis_index("seq")
    count = lax.axis_size("seq")
    on = [None]
    for offset in slot_offsets(index % 2)[1:]:
        inside = (index + offset >= 0) & (index + offset < count)
        on.append(inside & (mask[0, offset + W] == 1))
    row = 0
    for ref in (own, left, right, far, mate):
        n = ref.shape[1]
        kc[row : row + n] = ref[0]
        vc[row : row + n] = ref[1]
        row += n
    for s in range(NS):
        kt[:, s * BL : (s + 1) * BL] = kc[s * BL : (s + 1) * BL, :].T
    cols = [slice(i * HD, (i + 1) * HD) for i in range(G)]
    qp = jnp.concatenate([q[:, c] for c in cols], axis=0)
    gp = jnp.concatenate([grads[0][:, c] for c in cols], axis=0)
    for more in grads[1:]:
        gp = gp + jnp.concatenate([more[:, c] for c in cols], axis=0)
    s = lax.dot_general(kc[...], qp, NT, preferred_element_type=F32)
    pieces = [s[i * BL : (i + 1) * BL] for i in range(NS)]
    pieces = [p if f is None else jnp.where(f, p, -jnp.inf) for p, f in zip(pieces, on)]
    s = jnp.concatenate(pieces, axis=0)
    m = jnp.max(s, axis=0, keepdims=True)
    e = jnp.exp2((s - m) * (SCALE * LOG2E))
    p = e * (1.0 / jnp.sum(e, axis=0, keepdims=True))
    dp = lax.dot_general(vc[...], gp, NT, preferred_element_type=F32)
    delta = jnp.sum(p * dp, axis=0, keepdims=True)
    ds = (p * (dp - delta)).astype(B16)
    dv = lax.dot_general(p.astype(B16), gp, NN, preferred_element_type=F32)
    dk = lax.dot_general(ds, qp, NN, preferred_element_type=F32) * SCALE
    dqt = lax.dot_general(kt[...], ds, NN, preferred_element_type=F32)
    for i, c in enumerate(cols):
        dq[:, c] = (dqt[:, c].T * SCALE).astype(B16)
    for i, d in enumerate((dk, dv)):
        parts[i] = d[: 3 * BL]
        to_far[i] = d[3 * BL : 4 * BL].astype(B16)
        to_mate[i] = d[4 * BL :].astype(B16)


def attention_backward(mask, q, grads, slots, first, heads, kept):
    at = lambda h: (0, h + first)
    at3 = lambda h: (0, 0, h + first)
    here = lambda h: (0, h)
    width = HK * HD
    shapes = [((BL, HQ * HD), B16), ((2, 3 * BL, width), F32), ((2, 3 * BL, width), B16), ((2, BL, width), B16)]
    n_in = 2 + len(grads) + len(slots)
    return pl.pallas_call(
        functools.partial(backward_body, len(grads), len(kept)),
        grid=(heads,),
        in_specs=[pl.BlockSpec(memory_space=pltpu.SMEM), pl.BlockSpec((BL, G * HD), at)]
        + [pl.BlockSpec((BL, G * HD), here) for _ in grads]
        + [pl.BlockSpec((2, x.shape[1], HD), at3) for x in slots]
        + [pl.BlockSpec(memory_space=pl.ANY) for _ in kept],
        out_specs=[pl.BlockSpec((BL, G * HD), at)] + [pl.BlockSpec((2, s[1], HD), at3) for s, _ in shapes[1:]],
        out_shape=[jax.ShapeDtypeStruct(s, d) for s, d in shapes],
        scratch_shapes=[pltpu.VMEM((NS * BL, HD), B16), pltpu.VMEM((NS * BL, HD), B16), pltpu.VMEM((HD, NS * BL), B16)],
        input_output_aliases={n_in + i: i for i in range(len(kept))},
        compiler_params=pltpu.CompilerParams(vmem_limit_bytes=32 << 20),
        cost_estimate=pl.CostEstimate(flops=heads << 30, bytes_accessed=heads << 20, transcendentals=heads << 20),
        name="attention_backward",
    )(mask, q, *grads, *slots, *kept)


def join_body(k, v, out):
    out[0] = k[...]
    out[1] = v[...]


def join(k, v):
    return pl.pallas_call(
        join_body,
        out_shape=jax.ShapeDtypeStruct((2, *k.shape), k.dtype),
        compiler_params=pltpu.CompilerParams(vmem_limit_bytes=4 << 20),
        name="join",
    )(k, v)


def bundle_body(own, left, right, out):
    for i, ref in enumerate((own, left, right)):
        out[:, i * BL : (i + 1) * BL] = ref[...]


def bundle(own, left, right):
    n, rows, cols = own.shape
    return pl.pallas_call(
        bundle_body,
        out_shape=jax.ShapeDtypeStruct((n, 3 * rows, cols), own.dtype),
        compiler_params=pltpu.CompilerParams(vmem_limit_bytes=8 << 20),
        name="bundle",
    )(own, left, right)


def hold_body(*refs):
    pass


def hold(*arrays, flops=1 << 34):
    anywhere = [pl.BlockSpec(memory_space=pl.ANY) for _ in arrays]
    return pl.pallas_call(
        hold_body,
        in_specs=anywhere,
        out_specs=anywhere,
        out_shape=[jax.ShapeDtypeStruct(x.shape, x.dtype) for x in arrays],
        input_output_aliases={i: i for i in range(len(arrays))},
        compiler_params=pltpu.CompilerParams(vmem_limit_bytes=1 << 20),
        cost_estimate=pl.CostEstimate(flops=flops, bytes_accessed=0, transcendentals=0),
        name="hold",
    )(*arrays)


def shift_pairs(count, by):
    return [(i, i + by) for i in range(count) if 0 <= i + by < count]


def mate_pairs(count):
    return [(i, i ^ 1) for i in range(count)]


def far_pairs(count):
    ends = [(i, i + 3 if i % 2 else i - 3) for i in range(count)]
    return [(i, j) for i, j in ends if 0 <= j < count]


def shards(query_heads, key_heads, value_heads, section_cotangent, block_mask):
    sections = lax.axis_size("section")
    count = lax.axis_size("seq")
    half = HQ * HD // 2
    turn = sections // 2
    cot = section_cotangent[0]
    low, high = cot[:, :half], cot[:, half:]
    before = [(i, (i - 1) % sections) for i in range(sections)]
    own = join(key_heads[0], value_heads[0])
    left = lax.ppermute(own, "seq", shift_pairs(count, 2))
    right = lax.ppermute(own, "seq", shift_pairs(count, -2))
    far, grad_low = hold(
        lax.ppermute(own, "seq", far_pairs(count)), lax.ppermute(low, "section", before), flops=1 << 33
    )
    (turned,) = hold(lax.ppermute(high, "section", [(0, turn), (turn, 0)]), flops=1 << 33)
    left, right, late, _ = lax.optimization_barrier((left, right, high, turned))
    mate = lax.ppermute(bundle(own, left, right), "seq", mate_pairs(count))
    grad_high = lax.ppermute(late, "section", [(i, i - 1) for i in range(sections) if i % turn])
    grad_wrap = lax.ppermute(turned, "section", [(0, turn - 1), (turn, sections - 1)])
    slots = (own, left, right, far, mate)
    kept = attention_backward(block_mask, query_heads[0], (grad_low,), slots, 0, 2, ())
    grad_wrap, last = hold(grad_wrap, kept[3], flops=1 << 31)
    kept = [*kept[:3], last]
    query_grad, parts, to_mate, to_far = attention_backward(
        block_mask, query_heads[0], (grad_high, grad_wrap), slots, 2, 2, kept
    )
    (back_far,) = hold(lax.ppermute(to_far, "seq", far_pairs(count)), flops=1 << 33)
    sums = parts + lax.ppermute(to_mate, "seq", mate_pairs(count)).astype(F32)
    back_far, back_left, back_right = hold(
        back_far,
        lax.ppermute(sums[:, BL : 2 * BL].astype(B16), "seq", shift_pairs(count, -2)),
        lax.ppermute(sums[:, 2 * BL :].astype(B16), "seq", shift_pairs(count, 2)),
    )
    total = sums[:, :BL] + back_left.astype(F32) + back_right.astype(F32) + back_far.astype(F32)
    total = total.astype(B16)
    return query_grad[None], total[0][None], total[1][None]


def solution(mesh):
    in_specs = (
        P("section", "seq", None),
        P("section", "seq", None),
        P("section", "seq", None),
        P("section", "seq", None),
        P("seq", None),
    )
    out_specs = (P("section", "seq", None), P("section", "seq", None), P("section", "seq", None))
    return jax.shard_map(shards, mesh=mesh, in_specs=in_specs, out_specs=out_specs, check_vma=False)
```

```python
import functools
import math

import jax
import jax.numpy as jnp
from jax import lax
from jax.experimental import pallas as pl
from jax.experimental.pallas import tpu as pltpu
from jax.sharding import PartitionSpec as P

HQ, HK, HD, W = 32, 4, 128, 3
BL = 128
G = HQ // HK
NS = 2 * W + 1
SCALE = 1.0 / math.sqrt(HD)
LOG2E = math.log2(math.e)
NT = (((1,), (1,)), ((), ()))
NN = (((1,), (0,)), ((), ()))
F32, B16 = jnp.float32, jnp.bfloat16


def slot_offsets(odd):
    sign = 1 - 2 * odd
    return [0, -2, 2, -3 * sign, sign, sign - 2, sign + 2]


def backward_body(n_grads, n_kept, *refs):
    mask, q = refs[:2]
    grads = refs[2 : 2 + n_grads]
    own, left, right, far, mate = refs[2 + n_grads : 7 + n_grads]
    dq, parts, to_mate, to_far, kc, vc, kt = refs[7 + n_grads + n_kept :]
    index = lax.axis_index("seq")
    count = lax.axis_size("seq")
    on = [None]
    for offset in slot_offsets(index % 2)[1:]:
        inside = (index + offset >= 0) & (index + offset < count)
        on.append(inside & (mask[0, offset + W] == 1))
    row = 0
    for ref in (own, left, right, far, mate):
        n = ref.shape[1]
        kc[row : row + n] = ref[0]
        vc[row : row + n] = ref[1]
        row += n
    for s in range(NS):
        kt[:, s * BL : (s + 1) * BL] = kc[s * BL : (s + 1) * BL, :].T
    cols = [slice(i * HD, (i + 1) * HD) for i in range(G)]
    qp = jnp.concatenate([q[:, c] for c in cols], axis=0)
    gp = jnp.concatenate([grads[0][:, c] for c in cols], axis=0)
    for more in grads[1:]:
        gp = gp + jnp.concatenate([more[:, c] for c in cols], axis=0)
    s = lax.dot_general(kc[...], qp, NT, preferred_element_type=F32)
    pieces = [s[i * BL : (i + 1) * BL] for i in range(NS)]
    pieces = [p if f is None else jnp.where(f, p, -jnp.inf) for p, f in zip(pieces, on)]
    s = jnp.concatenate(pieces, axis=0)
    m = jnp.max(s, axis=0, keepdims=True)
    e = jnp.exp2((s - m) * (SCALE * LOG2E))
    p = e * (1.0 / jnp.sum(e, axis=0, keepdims=True))
    dp = lax.dot_general(vc[...], gp, NT, preferred_element_type=F32)
    delta = jnp.sum(p * dp, axis=0, keepdims=True)
    ds = (p * (dp - delta)).astype(B16)
    dv = lax.dot_general(p.astype(B16), gp, NN, preferred_element_type=F32)
    dk = lax.dot_general(ds, qp, NN, preferred_element_type=F32) * SCALE
    dqt = lax.dot_general(kt[...], ds, NN, preferred_element_type=F32)
    for i, c in enumerate(cols):
        dq[:, c] = (dqt[:, c].T * SCALE).astype(B16)
    for i, d in enumerate((dk, dv)):
        parts[i] = d[: 3 * BL]
        to_far[i] = d[3 * BL : 4 * BL].astype(B16)
        to_mate[i] = d[4 * BL :].astype(B16)


def attention_backward(mask, q, grads, slots, first, heads, kept):
    at = lambda h: (0, h + first)
    at3 = lambda h: (0, 0, h + first)
    here = lambda h: (0, h)
    width = HK * HD
    shapes = [((BL, HQ * HD), B16), ((2, 3 * BL, width), F32), ((2, 3 * BL, width), B16), ((2, BL, width), B16)]
    n_in = 2 + len(grads) + len(slots)
    return pl.pallas_call(
        functools.partial(backward_body, len(grads), len(kept)),
        grid=(heads,),
        in_specs=[pl.BlockSpec(memory_space=pltpu.SMEM), pl.BlockSpec((BL, G * HD), at)]
        + [pl.BlockSpec((BL, G * HD), here) for _ in grads]
        + [pl.BlockSpec((2, x.shape[1], HD), at3) for x in slots]
        + [pl.BlockSpec(memory_space=pl.ANY) for _ in kept],
        out_specs=[pl.BlockSpec((BL, G * HD), at)] + [pl.BlockSpec((2, s[1], HD), at3) for s, _ in shapes[1:]],
        out_shape=[jax.ShapeDtypeStruct(s, d) for s, d in shapes],
        scratch_shapes=[pltpu.VMEM((NS * BL, HD), B16), pltpu.VMEM((NS * BL, HD), B16), pltpu.VMEM((HD, NS * BL), B16)],
        input_output_aliases={n_in + i: i for i in range(len(kept))},
        compiler_params=pltpu.CompilerParams(vmem_limit_bytes=32 << 20),
        cost_estimate=pl.CostEstimate(flops=heads << 30, bytes_accessed=heads << 20, transcendentals=heads << 20),
        name="attention_backward",
    )(mask, q, *grads, *slots, *kept)


def join_body(k, v, out):
    out[0] = k[...]
    out[1] = v[...]


def join(k, v):
    return pl.pallas_call(
        join_body,
        out_shape=jax.ShapeDtypeStruct((2, *k.shape), k.dtype),
        compiler_params=pltpu.CompilerParams(vmem_limit_bytes=4 << 20),
        name="join",
    )(k, v)


def bundle_body(own, left, right, out):
    for i, ref in enumerate((own, left, right)):
        out[:, i * BL : (i + 1) * BL] = ref[...]


def bundle(own, left, right):
    n, rows, cols = own.shape
    return pl.pallas_call(
        bundle_body,
        out_shape=jax.ShapeDtypeStruct((n, 3 * rows, cols), own.dtype),
        compiler_params=pltpu.CompilerParams(vmem_limit_bytes=8 << 20),
        name="bundle",
    )(own, left, right)


def hold_body(*refs):
    pass


def hold(*arrays, flops=1 << 34):
    anywhere = [pl.BlockSpec(memory_space=pl.ANY) for _ in arrays]
    return pl.pallas_call(
        hold_body,
        in_specs=anywhere,
        out_specs=anywhere,
        out_shape=[jax.ShapeDtypeStruct(x.shape, x.dtype) for x in arrays],
        input_output_aliases={i: i for i in range(len(arrays))},
        compiler_params=pltpu.CompilerParams(vmem_limit_bytes=1 << 20),
        cost_estimate=pl.CostEstimate(flops=flops, bytes_accessed=0, transcendentals=0),
        name="hold",
    )(*arrays)


def shift_pairs(count, by):
    return [(i, i + by) for i in range(count) if 0 <= i + by < count]


def mate_pairs(count):
    return [(i, i ^ 1) for i in range(count)]


def far_pairs(count):
    ends = [(i, i + 3 if i % 2 else i - 3) for i in range(count)]
    return [(i, j) for i, j in ends if 0 <= j < count]


def shards(query_heads, key_heads, value_heads, section_cotangent, block_mask):
    sections = lax.axis_size("section")
    count = lax.axis_size("seq")
    half = HQ * HD // 2
    turn = sections // 2
    cot = section_cotangent[0]
    low, high = cot[:, :half], cot[:, half:]
    before = [(i, (i - 1) % sections) for i in range(sections)]
    own = join(key_heads[0], value_heads[0])
    left = lax.ppermute(own, "seq", shift_pairs(count, 2))
    right = lax.ppermute(own, "seq", shift_pairs(count, -2))
    far, grad_low = hold(
        lax.ppermute(own, "seq", far_pairs(count)), lax.ppermute(low, "section", [(i, i - 1) for i in range(sections) if i % turn]), flops=1 << 33
    )
    (turned,) = hold(lax.ppermute(low, "section", [(0, turn), (turn, 0)]), flops=1 << 33)
    left, right, late, _ = lax.optimization_barrier((left, right, high, turned))
    mate = lax.ppermute(bundle(own, left, right), "seq", mate_pairs(count))
    grad_high = lax.ppermute(late, "section", before)
    (grad_wrap,) = hold(lax.ppermute(turned, "section", [(0, turn - 1), (turn, sections - 1)]), flops=1 << 33)
    slots = (own, left, right, far, mate)
    kept = attention_backward(block_mask, query_heads[0], (grad_low, grad_wrap), slots, 0, 2, ())
    query_grad, parts, to_mate, to_far = attention_backward(
        block_mask, query_heads[0], (grad_high,), slots, 2, 2, kept
    )
    (back_far,) = hold(lax.ppermute(to_far, "seq", far_pairs(count)), flops=1 << 33)
    sums = parts + lax.ppermute(to_mate, "seq", mate_pairs(count)).astype(F32)
    back_far, back_left, back_right = hold(
        back_far,
        lax.ppermute(sums[:, BL : 2 * BL].astype(B16), "seq", shift_pairs(count, -2)),
        lax.ppermute(sums[:, 2 * BL :].astype(B16), "seq", shift_pairs(count, 2)),
    )
    total = sums[:, :BL] + back_left.astype(F32) + back_right.astype(F32) + back_far.astype(F32)
    total = total.astype(B16)
    return query_grad[None], total[0][None], total[1][None]


def solution(mesh):
    in_specs = (
        P("section", "seq", None),
        P("section", "seq", None),
        P("section", "seq", None),
        P("section", "seq", None),
        P("seq", None),
    )
    out_specs = (P("section", "seq", None), P("section", "seq", None), P("section", "seq", None))
    return jax.shard_map(shards, mesh=mesh, in_specs=in_specs, out_specs=out_specs, check_vma=False)
```

```python
import functools
import math

import jax
import jax.numpy as jnp
from jax import lax
from jax.experimental import pallas as pl
from jax.experimental.pallas import tpu as pltpu
from jax.sharding import PartitionSpec as P

HQ, HK, HD, W = 32, 4, 128, 3
BL = 128
G = HQ // HK
NS = 2 * W + 1
SCALE = 1.0 / math.sqrt(HD)
LOG2E = math.log2(math.e)
NT = (((1,), (1,)), ((), ()))
NN = (((1,), (0,)), ((), ()))
F32, B16 = jnp.float32, jnp.bfloat16


def slot_offsets(odd):
    sign = 1 - 2 * odd
    return [0, -2, 2, -3 * sign, sign, sign - 2, sign + 2]


def backward_body(n_grads, n_kept, *refs):
    mask, q = refs[:2]
    grads = refs[2 : 2 + n_grads]
    own, left, right, far, mate = refs[2 + n_grads : 7 + n_grads]
    dq, parts, to_mate, to_far, kc, vc, kt = refs[7 + n_grads + n_kept :]
    index = lax.axis_index("seq")
    count = lax.axis_size("seq")
    on = [None]
    for offset in slot_offsets(index % 2)[1:]:
        inside = (index + offset >= 0) & (index + offset < count)
        on.append(inside & (mask[0, offset + W] == 1))
    row = 0
    for ref in (own, left, right, far, mate):
        n = ref.shape[1]
        kc[row : row + n] = ref[0]
        vc[row : row + n] = ref[1]
        row += n
    for s in range(NS):
        kt[:, s * BL : (s + 1) * BL] = kc[s * BL : (s + 1) * BL, :].T
    cols = [slice(i * HD, (i + 1) * HD) for i in range(G)]
    qp = jnp.concatenate([q[:, c] for c in cols], axis=0)
    gp = jnp.concatenate([grads[0][:, c] for c in cols], axis=0)
    for more in grads[1:]:
        gp = gp + jnp.concatenate([more[:, c] for c in cols], axis=0)
    s = lax.dot_general(kc[...], qp, NT, preferred_element_type=F32)
    pieces = [s[i * BL : (i + 1) * BL] for i in range(NS)]
    pieces = [p if f is None else jnp.where(f, p, -jnp.inf) for p, f in zip(pieces, on)]
    s = jnp.concatenate(pieces, axis=0)
    m = jnp.max(s, axis=0, keepdims=True)
    e = jnp.exp2((s - m) * (SCALE * LOG2E))
    p = e * (1.0 / jnp.sum(e, axis=0, keepdims=True))
    dp = lax.dot_general(vc[...], gp, NT, preferred_element_type=F32)
    delta = jnp.sum(p * dp, axis=0, keepdims=True)
    ds = (p * (dp - delta)).astype(B16)
    dv = lax.dot_general(p.astype(B16), gp, NN, preferred_element_type=F32)
    dk = lax.dot_general(ds, qp, NN, preferred_element_type=F32) * SCALE
    dqt = lax.dot_general(kt[...], ds, NN, preferred_element_type=F32)
    for i, c in enumerate(cols):
        dq[:, c] = (dqt[:, c].T * SCALE).astype(B16)
    for i, d in enumerate((dk, dv)):
        parts[i] = d[: 3 * BL]
        to_far[i] = d[3 * BL : 4 * BL].astype(B16)
        to_mate[i] = d[4 * BL :].astype(B16)


def attention_backward(mask, q, grads, slots, first, heads, kept):
    at = lambda h: (0, h + first)
    at3 = lambda h: (0, 0, h + first)
    here = lambda h: (0, h)
    width = HK * HD
    shapes = [((BL, HQ * HD), B16), ((2, 3 * BL, width), F32), ((2, 3 * BL, width), B16), ((2, BL, width), B16)]
    n_in = 2 + len(grads) + len(slots)
    return pl.pallas_call(
        functools.partial(backward_body, len(grads), len(kept)),
        grid=(heads,),
        in_specs=[pl.BlockSpec(memory_space=pltpu.SMEM), pl.BlockSpec((BL, G * HD), at)]
        + [pl.BlockSpec((BL, G * HD), here) for _ in grads]
        + [pl.BlockSpec((2, x.shape[1], HD), at3) for x in slots]
        + [pl.BlockSpec(memory_space=pl.ANY) for _ in kept],
        out_specs=[pl.BlockSpec((BL, G * HD), at)] + [pl.BlockSpec((2, s[1], HD), at3) for s, _ in shapes[1:]],
        out_shape=[jax.ShapeDtypeStruct(s, d) for s, d in shapes],
        scratch_shapes=[pltpu.VMEM((NS * BL, HD), B16), pltpu.VMEM((NS * BL, HD), B16), pltpu.VMEM((HD, NS * BL), B16)],
        input_output_aliases={n_in + i: i for i in range(len(kept))},
        compiler_params=pltpu.CompilerParams(vmem_limit_bytes=32 << 20),
        cost_estimate=pl.CostEstimate(flops=heads << 30, bytes_accessed=heads << 20, transcendentals=heads << 20),
        name="attention_backward",
    )(mask, q, *grads, *slots, *kept)


def join_body(k, v, out):
    out[0] = k[...]
    out[1] = v[...]


def join(k, v):
    return pl.pallas_call(
        join_body,
        out_shape=jax.ShapeDtypeStruct((2, *k.shape), k.dtype),
        compiler_params=pltpu.CompilerParams(vmem_limit_bytes=4 << 20),
        name="join",
    )(k, v)


def bundle_body(own, left, right, out):
    for i, ref in enumerate((own, left, right)):
        out[:, i * BL : (i + 1) * BL] = ref[...]


def bundle(own, left, right):
    n, rows, cols = own.shape
    return pl.pallas_call(
        bundle_body,
        out_shape=jax.ShapeDtypeStruct((n, 3 * rows, cols), own.dtype),
        compiler_params=pltpu.CompilerParams(vmem_limit_bytes=8 << 20),
        name="bundle",
    )(own, left, right)


def hold_body(*refs):
    pass


def hold(*arrays, flops=1 << 34):
    anywhere = [pl.BlockSpec(memory_space=pl.ANY) for _ in arrays]
    return pl.pallas_call(
        hold_body,
        in_specs=anywhere,
        out_specs=anywhere,
        out_shape=[jax.ShapeDtypeStruct(x.shape, x.dtype) for x in arrays],
        input_output_aliases={i: i for i in range(len(arrays))},
        compiler_params=pltpu.CompilerParams(vmem_limit_bytes=1 << 20),
        cost_estimate=pl.CostEstimate(flops=flops, bytes_accessed=0, transcendentals=0),
        name="hold",
    )(*arrays)


def shift_pairs(count, by):
    return [(i, i + by) for i in range(count) if 0 <= i + by < count]


def mate_pairs(count):
    return [(i, i ^ 1) for i in range(count)]


def far_pairs(count):
    ends = [(i, i + 3 if i % 2 else i - 3) for i in range(count)]
    return [(i, j) for i, j in ends if 0 <= j < count]


def shards(query_heads, key_heads, value_heads, section_cotangent, block_mask):
    sections = lax.axis_size("section")
    count = lax.axis_size("seq")
    half = HQ * HD // 2
    turn = sections // 2
    cot = section_cotangent[0]
    low = cot[:, :half]
    before = [(i, (i - 1) % sections) for i in range(sections)]
    own = join(key_heads[0], value_heads[0])
    left = lax.ppermute(own, "seq", shift_pairs(count, 2))
    right = lax.ppermute(own, "seq", shift_pairs(count, -2))
    far, grad_low = hold(
        lax.ppermute(own, "seq", far_pairs(count)), lax.ppermute(low, "section", [(i, i - 1) for i in range(sections) if i % turn]), flops=1 << 33
    )
    (turned,) = hold(lax.ppermute(low, "section", [(0, turn), (turn, 0)]), flops=1 << 33)
    left, right, _ = lax.optimization_barrier((left, right, turned))
    mate = lax.ppermute(bundle(own, left, right), "seq", mate_pairs(count))
    mate, cot = lax.optimization_barrier((mate, cot))
    grad_high = lax.ppermute(cot[:, half:], "section", before)
    (grad_wrap,) = hold(lax.ppermute(turned, "section", [(0, turn - 1), (turn, sections - 1)]), flops=1 << 33)
    slots = (own, left, right, far, mate)
    kept = attention_backward(block_mask, query_heads[0], (grad_low, grad_wrap), slots, 0, 2, ())
    query_grad, parts, to_mate, to_far = attention_backward(
        block_mask, query_heads[0], (grad_high,), slots, 2, 2, kept
    )
    (back_far,) = hold(lax.ppermute(to_far, "seq", far_pairs(count)), flops=1 << 33)
    sums = parts + lax.ppermute(to_mate, "seq", mate_pairs(count)).astype(F32)
    back_far, back_left, back_right = hold(
        back_far,
        lax.ppermute(sums[:, BL : 2 * BL].astype(B16), "seq", shift_pairs(count, -2)),
        lax.ppermute(sums[:, 2 * BL :].astype(B16), "seq", shift_pairs(count, 2)),
    )
    total = sums[:, :BL] + back_left.astype(F32) + back_right.astype(F32) + back_far.astype(F32)
    total = total.astype(B16)
    return query_grad[None], total[0][None], total[1][None]


def solution(mesh):
    in_specs = (
        P("section", "seq", None),
        P("section", "seq", None),
        P("section", "seq", None),
        P("section", "seq", None),
        P("seq", None),
    )
    out_specs = (P("section", "seq", None), P("section", "seq", None), P("section", "seq", None))
    return jax.shard_map(shards, mesh=mesh, in_specs=in_specs, out_specs=out_specs, check_vma=False)
```

```python
import functools
import math

import jax
import jax.numpy as jnp
from jax import lax
from jax.experimental import pallas as pl
from jax.experimental.pallas import tpu as pltpu
from jax.sharding import PartitionSpec as P

HQ, HK, HD, W = 32, 4, 128, 3
BL = 128
G = HQ // HK
NS = 2 * W + 1
SCALE = 1.0 / math.sqrt(HD)
LOG2E = math.log2(math.e)
NT = (((1,), (1,)), ((), ()))
NN = (((1,), (0,)), ((), ()))
F32, B16 = jnp.float32, jnp.bfloat16


def slot_offsets(odd):
    sign = 1 - 2 * odd
    return [0, -2, 2, -3 * sign, sign, sign - 2, sign + 2]


def backward_body(n_grads, n_kept, *refs):
    mask, q = refs[:2]
    grads = refs[2 : 2 + n_grads]
    own, left, right, far, mate = refs[2 + n_grads : 7 + n_grads]
    dq, parts, to_mate, to_far, kc, vc, kt = refs[7 + n_grads + n_kept :]
    index = lax.axis_index("seq")
    count = lax.axis_size("seq")
    on = [None]
    for offset in slot_offsets(index % 2)[1:]:
        inside = (index + offset >= 0) & (index + offset < count)
        on.append(inside & (mask[0, offset + W] == 1))
    row = 0
    for ref in (own, left, right, far, mate):
        n = ref.shape[1]
        kc[row : row + n] = ref[0]
        vc[row : row + n] = ref[1]
        row += n
    for s in range(NS):
        kt[:, s * BL : (s + 1) * BL] = kc[s * BL : (s + 1) * BL, :].T
    cols = [slice(i * HD, (i + 1) * HD) for i in range(G)]
    qp = jnp.concatenate([q[:, c] for c in cols], axis=0)
    gp = jnp.concatenate([grads[0][:, c] for c in cols], axis=0)
    for more in grads[1:]:
        gp = gp + jnp.concatenate([more[:, c] for c in cols], axis=0)
    s = lax.dot_general(kc[...], qp, NT, preferred_element_type=F32)
    pieces = [s[i * BL : (i + 1) * BL] for i in range(NS)]
    pieces = [p if f is None else jnp.where(f, p, -jnp.inf) for p, f in zip(pieces, on)]
    s = jnp.concatenate(pieces, axis=0)
    m = jnp.max(s, axis=0, keepdims=True)
    e = jnp.exp2((s - m) * (SCALE * LOG2E))
    p = e * (1.0 / jnp.sum(e, axis=0, keepdims=True))
    dp = lax.dot_general(vc[...], gp, NT, preferred_element_type=F32)
    delta = jnp.sum(p * dp, axis=0, keepdims=True)
    ds = (p * (dp - delta)).astype(B16)
    dv = lax.dot_general(p.astype(B16), gp, NN, preferred_element_type=F32)
    dk = lax.dot_general(ds, qp, NN, preferred_element_type=F32) * SCALE
    dqt = lax.dot_general(kt[...], ds, NN, preferred_element_type=F32)
    for i, c in enumerate(cols):
        dq[:, c] = (dqt[:, c].T * SCALE).astype(B16)
    for i, d in enumerate((dk, dv)):
        parts[i] = d[: 3 * BL]
        to_far[i] = d[3 * BL : 4 * BL].astype(B16)
        to_mate[i] = d[4 * BL :].astype(B16)


def attention_backward(mask, q, grads, slots, first, heads, kept):
    at = lambda h: (0, h + first)
    at3 = lambda h: (0, 0, h + first)
    here = lambda h: (0, h)
    width = HK * HD
    shapes = [((BL, HQ * HD), B16), ((2, 3 * BL, width), F32), ((2, 3 * BL, width), B16), ((2, BL, width), B16)]
    n_in = 2 + len(grads) + len(slots)
    return pl.pallas_call(
        functools.partial(backward_body, len(grads), len(kept)),
        grid=(heads,),
        in_specs=[pl.BlockSpec(memory_space=pltpu.SMEM), pl.BlockSpec((BL, G * HD), at)]
        + [pl.BlockSpec((BL, G * HD), here) for _ in grads]
        + [pl.BlockSpec((2, x.shape[1], HD), at3) for x in slots]
        + [pl.BlockSpec(memory_space=pl.ANY) for _ in kept],
        out_specs=[pl.BlockSpec((BL, G * HD), at)] + [pl.BlockSpec((2, s[1], HD), at3) for s, _ in shapes[1:]],
        out_shape=[jax.ShapeDtypeStruct(s, d) for s, d in shapes],
        scratch_shapes=[pltpu.VMEM((NS * BL, HD), B16), pltpu.VMEM((NS * BL, HD), B16), pltpu.VMEM((HD, NS * BL), B16)],
        input_output_aliases={n_in + i: i for i in range(len(kept))},
        compiler_params=pltpu.CompilerParams(vmem_limit_bytes=32 << 20),
        cost_estimate=pl.CostEstimate(flops=heads << 30, bytes_accessed=heads << 20, transcendentals=heads << 20),
        name="attention_backward",
    )(mask, q, *grads, *slots, *kept)


def join_body(k, v, out):
    out[0] = k[...]
    out[1] = v[...]


def join(k, v):
    return pl.pallas_call(
        join_body,
        out_shape=jax.ShapeDtypeStruct((2, *k.shape), k.dtype),
        compiler_params=pltpu.CompilerParams(vmem_limit_bytes=4 << 20),
        name="join",
    )(k, v)


def bundle_body(own, left, right, out):
    for i, ref in enumerate((own, left, right)):
        out[:, i * BL : (i + 1) * BL] = ref[...]


def bundle(own, left, right):
    n, rows, cols = own.shape
    return pl.pallas_call(
        bundle_body,
        out_shape=jax.ShapeDtypeStruct((n, 3 * rows, cols), own.dtype),
        compiler_params=pltpu.CompilerParams(vmem_limit_bytes=8 << 20),
        name="bundle",
    )(own, left, right)


def hold_body(*refs):
    pass


def hold(*arrays, flops=1 << 34):
    anywhere = [pl.BlockSpec(memory_space=pl.ANY) for _ in arrays]
    return pl.pallas_call(
        hold_body,
        in_specs=anywhere,
        out_specs=anywhere,
        out_shape=[jax.ShapeDtypeStruct(x.shape, x.dtype) for x in arrays],
        input_output_aliases={i: i for i in range(len(arrays))},
        compiler_params=pltpu.CompilerParams(vmem_limit_bytes=1 << 20),
        cost_estimate=pl.CostEstimate(flops=flops, bytes_accessed=0, transcendentals=0),
        name="hold",
    )(*arrays)


def shift_pairs(count, by):
    return [(i, i + by) for i in range(count) if 0 <= i + by < count]


def mate_pairs(count):
    return [(i, i ^ 1) for i in range(count)]


def far_pairs(count):
    ends = [(i, i + 3 if i % 2 else i - 3) for i in range(count)]
    return [(i, j) for i, j in ends if 0 <= j < count]


def shards(query_heads, key_heads, value_heads, section_cotangent, block_mask):
    sections = lax.axis_size("section")
    count = lax.axis_size("seq")
    half = HQ * HD // 2
    turn = sections // 2
    cot = section_cotangent[0]
    low = cot[:, :half]
    before = [(i, (i - 1) % sections) for i in range(sections)]
    own = join(key_heads[0], value_heads[0])
    left = lax.ppermute(own, "seq", shift_pairs(count, 2))
    right = lax.ppermute(own, "seq", shift_pairs(count, -2))
    far, grad_low = hold(
        lax.ppermute(own, "seq", far_pairs(count)), lax.ppermute(low, "section", [(i, i - 1) for i in range(sections) if i % turn]), flops=1 << 33
    )
    (turned,) = hold(lax.ppermute(low, "section", [(0, turn), (turn, 0)]), flops=1 << 33)
    left, right, _ = lax.optimization_barrier((left, right, turned))
    joined, cot = lax.optimization_barrier((bundle(own, left, right), cot))
    (mate,) = hold(lax.ppermute(joined, "seq", mate_pairs(count)), flops=1 << 32)
    grad_high = lax.ppermute(cot[:, half:], "section", before)
    (grad_wrap,) = hold(lax.ppermute(turned, "section", [(0, turn - 1), (turn, sections - 1)]), flops=1 << 33)
    slots = (own, left, right, far, mate)
    kept = attention_backward(block_mask, query_heads[0], (grad_low, grad_wrap), slots, 0, 2, ())
    query_grad, parts, to_mate, to_far = attention_backward(
        block_mask, query_heads[0], (grad_high,), slots, 2, 2, kept
    )
    (back_far,) = hold(lax.ppermute(to_far, "seq", far_pairs(count)), flops=1 << 33)
    sums = parts + lax.ppermute(to_mate, "seq", mate_pairs(count)).astype(F32)
    back_far, back_left, back_right = hold(
        back_far,
        lax.ppermute(sums[:, BL : 2 * BL].astype(B16), "seq", shift_pairs(count, -2)),
        lax.ppermute(sums[:, 2 * BL :].astype(B16), "seq", shift_pairs(count, 2)),
    )
    total = sums[:, :BL] + back_left.astype(F32) + back_right.astype(F32) + back_far.astype(F32)
    total = total.astype(B16)
    return query_grad[None], total[0][None], total[1][None]


def solution(mesh):
    in_specs = (
        P("section", "seq", None),
        P("section", "seq", None),
        P("section", "seq", None),
        P("section", "seq", None),
        P("seq", None),
    )
    out_specs = (P("section", "seq", None), P("section", "seq", None), P("section", "seq", None))
    return jax.shard_map(shards, mesh=mesh, in_specs=in_specs, out_specs=out_specs, check_vma=False)
```
